256 devices in a mesh: sub: 32 (over x, z), vec: 8 (over y, core).
Axes of the slice: x: 4, y: 4, z: 8, core: 2. Of those that a mesh axis runs over, the one named last changes fastest.
Arguments:
- coefficients: bfloat16 [1024, 20480], P('sub', 'vec'), may hold values from -6 to 6
- row_counts: int32 [32], replicated, may hold values from 1 to 1024, 16384 in all
- ancestors: int32 [32, 3], replicated, may hold values from 0 to 27, as said below
- interior_modes: bfloat16 [131072, 1024], P('sub'), may hold values from -0.25 to 0.25
- separator_modes: bfloat16 [8192, 128], replicated, may hold values from -0.5 to 0.5
- coupling: bfloat16 [131072, 768], P('sub'), may hold values from -0.3125 to 0.3125
- pattern: int32 [32, 16, 3], P('sub'), may hold values 0 or 1
Outputs:
- interior_field: bfloat16 [131072, 1024], P('sub', 'vec')
- separator_field: bfloat16 [8192, 1024], P('sub', 'vec')
The draws below stay inside these ranges and needn't reach their ends.
Inputs may be any that keep to these rules, and one draw needn't show every extreme that they name: `ancestors`: the separators form binary trees: substructures pair under level-1 separators, pairs of those under level-2 separators, and so on, so that a level-l separator lies over 2**l substructures; no separator appears at two levels. `row_counts`: the counts sum to 512 * 32.
All inputs are finite; a program needn't handle non-finite values. No bound on the sum of `pattern` on one device may be relied on, other than what follows from the above.
Results may differ from the reference program's by a relative error of at most 0.0038.
Values may be sent and summed in bfloat16 or wider, within the bound.
A program may use at most 128 MiB of HBM per device.

```python
import math
import jax
import jax.numpy as jnp
import numpy as np
from jax import lax

K = 1024
BW = 256
SEPM = 128
LEVELS = 3
ROWS_MEAN = 512
PHYS = 4096
CAP = 1024
NBLK = 16
M = 20480
N_SUB = 32
N_VEC = 8


def draw_ancestors(key, part):
    leaf_place = jax.random.permutation(jax.random.fold_in(key, 11), N_SUB)
    labels = jax.random.permutation(jax.random.fold_in(key, 12), 7 * N_SUB // 8)
    level_one = labels[leaf_place // 2]
    level_two = labels[N_SUB // 2 + leaf_place // 4]
    level_three = labels[3 * N_SUB // 4 + leaf_place // 8]
    return jnp.stack([level_one, level_two, level_three], axis=1).astype(jnp.int32)


def touch_ends(array, own_key, smallest, top_value):
    longest = array.shape.index(max(array.shape))
    spots = []
    for shift in (0, 1):
        where = [jax.random.randint(jax.random.fold_in(own_key, axis), (), 0, length) for axis, length in enumerate(array.shape)]
        where[longest] = (where[longest] + shift) % array.shape[longest]
        spots.append(tuple(where))
    return array.at[spots[0]].set(smallest).at[spots[1]].set(top_value)


def block_scale(own_key, dims, split, smallest, high):
    def one(dim, blocks):
        heights = jax.random.uniform(jax.random.fold_in(jax.random.fold_in(own_key, 6), dim), (blocks,), jnp.float32, smallest / len(split), high / len(split))
        return jnp.repeat(jnp.exp(heights), dims[dim] // blocks).reshape((-1,) + (1,) * (len(dims) - dim - 1))

    gain = one(*split[0])
    for cut in split[1:]:
        gain = gain * one(*cut)
    return gain


def profile(count, total, limit, skew):
    weights = [(1 << 20) // math.isqrt(grade ** skew) + 1 for grade in range(2, count + 1)]
    surplus, holding = total - limit - (count - 1), [1] * (count - 1)
    while surplus > 0:
        candidates = [i for i in range(count - 1) if holding[i] < limit]
        whole, budget = sum([weights[i] for i in candidates]), surplus
        for i in candidates:
            addition = min(limit - holding[i], max(1, budget * weights[i] // whole), surplus)
            holding[i] = holding[i] + addition
            surplus = surplus - addition
    return np.array([limit] + holding)


def ragged_sizes(own_key, number_of, total, most, slope):
    if number_of == 2:
        one = jax.random.randint(own_key, (), max(1, total - most), min(most, total - 1) + 1)
        return jnp.stack([one, total - one])
    lengths = jnp.asarray(profile(number_of, total, most, slope), jnp.int32)
    couples = (number_of - 1) // 2
    donor, receiver = lengths[1:1 + 2 * couples:2], lengths[2:2 + 2 * couples:2]
    slack = jnp.minimum(donor - 1, most - receiver)
    moved = jax.random.randint(jax.random.fold_in(own_key, 1), (couples,), 0, 1 << 20) % (slack + 1)
    lengths = lengths.at[1:1 + 2 * couples:2].set(donor - moved).at[2:2 + 2 * couples:2].set(receiver + moved)
    return lengths[jax.random.permutation(jax.random.fold_in(own_key, 2), number_of)]


def bell_draw(key, extent, width, bound, cuts=(), kind=jnp.bfloat16):
    array = jax.random.normal(key, extent, jnp.float32) * width
    if len(cuts) > 0:
        array = block_scale(key, extent, cuts, -0.22, 0.18) * array
    return jnp.clip(array, min=-bound, max=bound).astype(kind)


def setup_inputs(seed: int = 0) -> dict:
    streams_of = jax.random.split(jax.random.key(seed), 8)
    return {
        "coefficients": bell_draw(streams_of[0], (K, M), 1.0, 6.0, ((0, 32), (1, 8))),
        "row_counts": ragged_sizes(streams_of[1], N_SUB, ROWS_MEAN * N_SUB, 2 * ROWS_MEAN, 2).astype(jnp.int32),
        "ancestors": draw_ancestors(jax.random.fold_in(streams_of[7], 71), 0),
        "interior_modes": bell_draw(streams_of[3], (N_SUB * PHYS, CAP), ROWS_MEAN ** -0.5, 0.25, ((0, 32),)),
        "separator_modes": bell_draw(streams_of[4], (N_SUB * BW, SEPM), SEPM ** -0.5, 0.5),
        "coupling": bell_draw(streams_of[5], (N_SUB * PHYS, LEVELS * BW), (LEVELS * BW // 2) ** -0.5, 0.3125, ((0, 32),)),
        "pattern": touch_ends((jax.random.randint(streams_of[6], (N_SUB, NBLK, LEVELS), 0, 2) < 1).astype(jnp.int32), jax.random.fold_in(streams_of[6], 1), 0, 1),
    }


def reference(coefficients, row_counts, ancestors, interior_modes, separator_modes, coupling, pattern):
    ordered = coefficients.reshape(N_SUB, N_VEC, K // (N_SUB * N_VEC), M)
    ordered = jnp.transpose(ordered, (1, 0, 2, 3)).reshape(K, M)
    offsets = (jnp.cumsum(row_counts) - row_counts).astype(jnp.int32)
    interior_total = ROWS_MEAN * N_SUB
    contract = (((1,), (1,)), ((), ()))

    def separator_one(index):
        start = (interior_total + index * SEPM).astype(jnp.int32)
        sep_coef = lax.dynamic_slice_in_dim(ordered, start, SEPM, 1)
        modes = lax.dynamic_slice_in_dim(separator_modes, (index * BW).astype(jnp.int32), BW, 0)
        return lax.dot_general(modes, sep_coef, contract, preferred_element_type=jnp.float32).astype(jnp.bfloat16)

    owners = jnp.arange(N_SUB, dtype=jnp.int32)
    separated = lax.map(separator_one, owners)

    def owner_one(index):
        positions = jnp.arange(CAP, dtype=jnp.int32)
        live = positions < row_counts[index]
        row_index = jnp.where(live, offsets[index] + positions, 0).astype(jnp.int32)
        picked = jnp.take(ordered, row_index, axis=1)
        picked = jnp.where(live[None, :], picked, jnp.zeros((), picked.dtype))
        modes = lax.dynamic_slice_in_dim(interior_modes, (index * PHYS).astype(jnp.int32), PHYS, 0)
        total = lax.dot_general(modes, picked, contract, preferred_element_type=jnp.float32)
        block = lax.dynamic_slice_in_dim(coupling, (index * PHYS).astype(jnp.int32), PHYS, 0)
        gates = pattern[index].astype(block.dtype)
        masked = (block.reshape(PHYS // BW, BW, LEVELS, BW) * gates[:, None, :, None]).reshape(PHYS, LEVELS * BW)
        above = jnp.take(separated, ancestors[index], axis=0).reshape(LEVELS * BW, K)
        total = total + jnp.dot(masked, above, preferred_element_type=jnp.float32)
        return total.astype(jnp.bfloat16)

    interior_field = lax.map(owner_one, owners).reshape(N_SUB * PHYS, K)
    separator_field = separated.reshape(N_SUB * BW, K)
    return interior_field, separator_field
```

```python
import jax
import jax.numpy as jnp
from jax import lax
from jax.experimental import pallas as pl
from jax.experimental.pallas import tpu as pltpu
from jax.sharding import PartitionSpec as P

BW = 256
SEPM = 128
LEVELS = 3
N_SUB = 32
N_Z = 8
N_VEC = 8
ROWS = 4
TILES_A = 20
TILES_I = 128
WIN = 9
SEPS = 1 + LEVELS
CAP = 1024
PHYS = 4096
NBLK = PHYS // BW
MESH = pl.DeviceIdType.MESH
BF16 = jnp.bfloat16
F32 = jnp.float32
NT = (((1,), (1,)), ((), ()))


def kernel(
    counts,
    ancestors,
    gates,
    coef_hbm,
    modes_hbm,
    sep_hbm,
    coupling_hbm,
    out,
    field,
    coef,
    modes,
    sep,
    coupling,
    send_a,
    recv_a,
    send_s,
    recv_s,
    send_w,
    recv_w,
    sep_coef,
    win_coef,
    above,
    total,
    weights,
    load_sem,
    send_a_sem,
    recv_a_sem,
    send_s_sem,
    recv_s_sem,
    send_w_sem,
    recv_w_sem,
):
    me = lax.axis_index("sub")
    mv = lax.axis_index("vec")
    barrier = pltpu.get_barrier_semaphore()

    def greet_vec(i, c):
        pl.semaphore_signal(
            barrier, inc=1, device_id={"vec": lax.rem(mv + i, N_VEC)}, device_id_type=MESH
        )
        return c

    def greet_sub(i, c):
        pl.semaphore_signal(
            barrier, inc=1, device_id={"sub": lax.rem(me + i, N_SUB)}, device_id_type=MESH
        )
        return c

    lax.fori_loop(1, N_VEC, greet_vec, 0)
    lax.fori_loop(1, N_SUB, greet_sub, 0)

    load_coef = pltpu.make_async_copy(coef_hbm, coef, load_sem.at[0])
    load_sep = pltpu.make_async_copy(sep_hbm, sep, load_sem.at[1])
    load_coupling = pltpu.make_async_copy(coupling_hbm, coupling, load_sem.at[2])
    load_modes = pltpu.make_async_copy(modes_hbm, modes, load_sem.at[3])
    load_coef.start()
    load_coef.wait()

    def split_rows(t, c):
        cols = pl.ds(pl.multiple_of(t * 128, 128), 128)
        for v in range(N_VEC):
            send_a[v, t] = coef[ROWS * v : ROWS * (v + 1), cols]
        return c

    lax.fori_loop(0, TILES_A, split_rows, 0)
    load_sep.start()
    load_coupling.start()
    load_modes.start()
    pl.semaphore_wait(barrier, N_VEC + N_SUB - 2)

    def copy_a(v):
        return pltpu.make_async_remote_copy(
            src_ref=send_a.at[v],
            dst_ref=recv_a.at[pl.ds(mv * TILES_A, TILES_A)],
            send_sem=send_a_sem.at[v],
            recv_sem=recv_a_sem.at[mv],
            device_id={"vec": v},
            device_id_type=MESH,
        )

    def own_a():
        return pltpu.make_async_copy(
            send_a.at[mv], recv_a.at[pl.ds(mv * TILES_A, TILES_A)], recv_a_sem.at[mv]
        )

    def start_a(i, c):
        copy_a(lax.rem(mv + i, N_VEC)).start()
        return c

    lax.fori_loop(1, N_VEC, start_a, 0)
    own_a().start()

    def wait_a(v, c):
        pltpu.make_async_copy(
            recv_a.at[pl.ds(v * TILES_A, TILES_A)],
            recv_a.at[pl.ds(v * TILES_A, TILES_A)],
            recv_a_sem.at[v],
        ).wait()
        return c

    lax.fori_loop(0, N_VEC, wait_a, 0)

    for s in range(N_SUB):
        send_s[s, 0] = recv_a[TILES_I + s]
        for l in range(LEVELS):
            send_s[s, 1 + l] = recv_a[TILES_I + ancestors[l, s]]

    def target(i):
        j = i // 4
        h = (j + 1) // 2
        dz = lax.rem(4 + h * (1 - 2 * lax.rem(j, 2)), N_Z)
        dx = lax.rem(i, 4)
        x = lax.rem(me // N_Z + dx, N_SUB // N_Z)
        z = lax.rem(lax.rem(me, N_Z) + dz, N_Z)
        return x * N_Z + z

    def remote(src, dst, ssem, rsem, s):
        return pltpu.make_async_remote_copy(
            src_ref=src.at[s],
            dst_ref=dst.at[me],
            send_sem=ssem.at[s],
            recv_sem=rsem.at[me],
            device_id={"sub": s},
            device_id_type=MESH,
        )

    def start_s(i, c):
        remote(send_s, recv_s, send_s_sem, recv_s_sem, target(i)).start()
        return c

    lax.fori_loop(0, N_SUB - 4, start_s, 0)
    lax.fori_loop(N_SUB - 3, N_SUB, start_s, 0)
    pltpu.make_async_copy(send_s.at[me], recv_s.at[me], recv_s_sem.at[me]).start()

    offset = jnp.int32(0)
    my_off = jnp.int32(0)
    for s in range(N_SUB):
        send_w[s] = recv_a[pl.ds(offset >> 7, WIN)]
        my_off = my_off + jnp.where(s < me, counts[s], 0)
        offset = offset + counts[s]

    def start_w(i, c):
        remote(send_w, recv_w, send_w_sem, recv_w_sem, target(i)).start()
        return c

    lax.fori_loop(0, N_SUB - 4, start_w, 0)
    lax.fori_loop(N_SUB - 3, N_SUB, start_w, 0)
    pltpu.make_async_copy(send_w.at[me], recv_w.at[me], recv_w_sem.at[me]).start()

    def gather_s(g, c):
        for q in range(4):
            s = g * 4 + q
            pltpu.make_async_copy(recv_s.at[s], recv_s.at[s], recv_s_sem.at[s]).wait()
            for t in range(SEPS):
                sep_coef[g, ROWS * q : ROWS * (q + 1), t * 128 : (t + 1) * 128] = recv_s[s, t]
        return c

    lax.fori_loop(0, N_SUB // 4, gather_s, 0)
    load_sep.wait()

    def field_of(index, t):
        block = sep_coef[:, :, t * 128 : (t + 1) * 128].reshape(128, 128)
        rows = sep[index]
        return lax.dot_general(rows, block, NT, preferred_element_type=F32).astype(BF16)

    field[...] = field_of(me, 0)
    for l in range(LEVELS):
        above[l * BW : (l + 1) * BW, :] = field_of(ancestors[l, me], 1 + l)
    load_coupling.wait()

    def couple(b, c):
        rows = pl.ds(pl.multiple_of(b * BW, BW), BW)
        acc = jnp.zeros((BW, 128), F32)
        for l in range(LEVELS):
            gate = gates[l, 0, b].astype(F32)
            acc = acc + gate * jnp.dot(
                coupling[rows, l * BW : (l + 1) * BW],
                above[l * BW : (l + 1) * BW, :],
                preferred_element_type=F32,
            )
        total[rows, :] = acc
        return c

    lax.fori_loop(0, NBLK, couple, 0)

    my_count = counts[me]
    shift = my_off & 127

    def gather_w(g, c):
        for q in range(4):
            s = g * 4 + q
            pltpu.make_async_copy(recv_w.at[s], recv_w.at[s], recv_w_sem.at[s]).wait()
            for t in range(WIN):
                win_coef[g, ROWS * q : ROWS * (q + 1), t * 128 : (t + 1) * 128] = recv_w[s, t]
        return c

    lax.fori_loop(0, N_SUB // 4, gather_w, 0)
    row = lax.broadcasted_iota(jnp.int32, (128, 256), 0)
    col = lax.broadcasted_iota(jnp.int32, (128, 256), 1)
    for t in range(CAP // 128):
        pick = jnp.where((col == row + shift) & (row + t * 128 < my_count), 1.0, 0.0).astype(BF16)
        pair = win_coef[:, :, t * 128 : (t + 2) * 128].reshape(128, 256)
        weights[t * 128 : (t + 1) * 128, :] = lax.dot_general(
            pick, pair, NT, preferred_element_type=F32
        ).astype(BF16)
    load_modes.wait()

    def finish(b, c):
        rows = pl.ds(pl.multiple_of(b * 512, 512), 512)
        part = jnp.dot(modes[rows, :], weights[...], preferred_element_type=F32)
        out[rows, :] = (total[rows, :] + part).astype(BF16)
        return c

    lax.fori_loop(0, PHYS // 512, finish, 0)

    def drain_a(i, c):
        copy_a(lax.rem(mv + i, N_VEC)).wait_send()
        return c

    def drain_b(i, c):
        s = lax.rem(me + i, N_SUB)
        remote(send_s, recv_s, send_s_sem, recv_s_sem, s).wait_send()
        remote(send_w, recv_w, send_w_sem, recv_w_sem, s).wait_send()
        return c

    lax.fori_loop(1, N_VEC, drain_a, 0)
    lax.fori_loop(1, N_SUB, drain_b, 0)


def body(coefficients, row_counts, ancestors, interior_modes, separator_modes, coupling, pattern):
    smem = pl.BlockSpec(memory_space=pltpu.SMEM)
    hbm = pl.BlockSpec(memory_space=pl.ANY)
    vmem = pl.BlockSpec(memory_space=pltpu.VMEM)
    dma = pltpu.SemaphoreType.DMA
    return pl.pallas_call(
        kernel,
        out_shape=(
            jax.ShapeDtypeStruct((PHYS, 128), BF16),
            jax.ShapeDtypeStruct((BW, 128), BF16),
        ),
        in_specs=[smem, smem, smem, hbm, hbm, hbm, hbm],
        out_specs=(vmem, vmem),
        scratch_shapes=[
            pltpu.VMEM((ROWS * N_VEC, TILES_A * 128), BF16),
            pltpu.VMEM((PHYS, CAP), BF16),
            pltpu.VMEM((N_SUB, BW, SEPM), BF16),
            pltpu.VMEM((PHYS, LEVELS * BW), BF16),
            pltpu.VMEM((N_VEC, TILES_A, ROWS, 128), BF16),
            pltpu.VMEM((N_VEC * TILES_A, ROWS, 128), BF16),
            pltpu.VMEM((N_SUB, SEPS, ROWS, 128), BF16),
            pltpu.VMEM((N_SUB, SEPS, ROWS, 128), BF16),
            pltpu.VMEM((N_SUB, WIN, ROWS, 128), BF16),
            pltpu.VMEM((N_SUB, WIN, ROWS, 128), BF16),
            pltpu.VMEM((N_SUB // 4, 4 * ROWS, SEPS * 128), BF16),
            pltpu.VMEM((N_SUB // 4, 4 * ROWS, WIN * 128), BF16),
            pltpu.VMEM((LEVELS * BW, 128), BF16),
            pltpu.VMEM((PHYS, 128), F32),
            pltpu.VMEM((CAP, 128), BF16),
            dma((4,)),
            dma((N_VEC,)),
            dma((N_VEC,)),
            dma((N_SUB,)),
            dma((N_SUB,)),
            dma((N_SUB,)),
            dma((N_SUB,)),
        ],
        compiler_params=pltpu.CompilerParams(
            collective_id=0, has_side_effects=True, vmem_limit_bytes=60 * 1024 * 1024
        ),
        name="recover",
    )(
        row_counts,
        ancestors.T,
        jnp.transpose(pattern, (2, 0, 1)),
        coefficients,
        interior_modes,
        separator_modes.reshape(N_SUB, BW, SEPM),
        coupling,
    )


def solution(mesh):
    placed = (P("sub", "vec"), P(), P(), P("sub", None), P(), P("sub", None), P("sub", None, None))
    return jax.shard_map(
        body,
        mesh=mesh,
        in_specs=placed,
        out_specs=(P("sub", "vec"), P("sub", "vec")),
        check_vma=False,
    )
```

```python
import jax
import jax.numpy as jnp
from jax import lax
from jax.experimental import pallas as pl
from jax.experimental.pallas import tpu as pltpu
from jax.sharding import PartitionSpec as P

BW = 256
SEPM = 128
LEVELS = 3
N_SUB = 32
N_X = 4
N_Z = 8
N_VEC = 8
ROWS = 4
TILES_A = 20
TILES_I = 128
SEPS = 1 + LEVELS
WIN = 9
GROUPS = ((0, SEPS), (SEPS, 5), (SEPS + 5, 2), (SEPS + 7, 2))
CHUNKS = ((0, 4), (4, 2), (6, 2))
SLOT = SEPS + WIN
CAP = 1024
PHYS = 4096
NBLK = PHYS // BW
MESH = pl.DeviceIdType.MESH
BF16 = jnp.bfloat16
F32 = jnp.float32
NT = (((1,), (1,)), ((), ()))


def kernel(
    counts_hbm,
    ancestors_hbm,
    gates_hbm,
    coef_hbm,
    modes_hbm,
    sep_hbm,
    coupling_hbm,
    out,
    field,
    counts,
    ancestors,
    gates,
    coef,
    modes,
    sep,
    coupling,
    send_a,
    recv_a,
    send_b,
    recv_b,
    lanes,
    above,
    total,
    weights,
    load_sem,
    send_a_sem,
    recv_a_sem,
    send_b_sem,
    recv_b_sem,
    relay_sem,
):
    me = lax.axis_index("sub")
    mv = lax.axis_index("vec")
    mx = lax.div(me, N_Z)
    mz = lax.rem(me, N_Z)
    z_up = mx * N_Z + lax.rem(mz + 1, N_Z)
    z_down = mx * N_Z + lax.rem(mz + N_Z - 1, N_Z)
    x_up = lax.rem(mx + 1, N_X) * N_Z + mz
    x_down = lax.rem(mx + N_X - 1, N_X) * N_Z + mz

    def load(src, dst, i):
        return pltpu.make_async_copy(src, dst, load_sem.at[i])

    load_coef = load(coef_hbm, coef, 0)
    load_sep = load(sep_hbm, sep, 1)
    load_coupling = load(coupling_hbm, coupling, 2)
    load_modes = load(modes_hbm, modes, 3)
    load_counts = load(counts_hbm, counts, 4)
    load_ancestors = load(ancestors_hbm, ancestors, 5)
    load_gates = load(gates_hbm, gates, 6)

    barrier = pltpu.get_barrier_semaphore()
    for i in range(1, N_VEC):
        pl.semaphore_signal(
            barrier, inc=1, device_id={"vec": lax.rem(mv + i, N_VEC)}, device_id_type=MESH
        )
    for s in (z_up, z_down, x_up, x_down):
        pl.semaphore_signal(barrier, inc=1, device_id={"sub": s}, device_id_type=MESH)
    load_coef.start()
    load_counts.start()
    load_ancestors.start()
    load_gates.start()
    load_sep.start()
    load_coupling.start()
    load_modes.start()
    load_coef.wait()

    def split_rows(t, c):
        cols = pl.ds(pl.multiple_of(t * 128, 128), 128)
        for v in range(N_VEC):
            send_a[v, t] = coef[ROWS * v : ROWS * (v + 1), cols]
        return c

    lax.fori_loop(0, TILES_A, split_rows, 0)
    pl.semaphore_wait(barrier, N_VEC - 1 + 4)

    def copy_a(v):
        return pltpu.make_async_remote_copy(
            src_ref=send_a.at[v],
            dst_ref=recv_a.at[pl.ds(mv * TILES_A, TILES_A)],
            send_sem=send_a_sem.at[v],
            recv_sem=recv_a_sem.at[mv],
            device_id={"vec": v},
            device_id_type=MESH,
        )

    def start_a(i, c):
        copy_a(lax.rem(mv + i, N_VEC)).start()
        return c

    lax.fori_loop(1, N_VEC, start_a, 0)
    pltpu.make_async_copy(
        send_a.at[mv], recv_a.at[pl.ds(mv * TILES_A, TILES_A)], recv_a_sem.at[mv]
    ).start()

    for r in range(5):
        up, down = (z_up, z_down) if r < 3 else (x_up, x_down)
        pl.semaphore_signal(
            relay_sem.at[2 * r], inc=1, device_id={"sub": up}, device_id_type=MESH
        )
        pl.semaphore_signal(
            relay_sem.at[2 * r + 1], inc=1, device_id={"sub": down}, device_id_type=MESH
        )
        pl.semaphore_wait(relay_sem.at[2 * r], 1)
        pl.semaphore_wait(relay_sem.at[2 * r + 1], 1)

    load_counts.wait()
    load_ancestors.wait()
    load_gates.wait()

    def wait_a(v, c):
        block = recv_a.at[pl.ds(v * TILES_A, TILES_A)]
        pltpu.make_async_copy(block, block, recv_a_sem.at[v]).wait()
        return c

    lax.fori_loop(0, N_VEC, wait_a, 0)

    def remote(g, s):
        start, size = GROUPS[g]
        return pltpu.make_async_remote_copy(
            src_ref=send_b.at[s, pl.ds(start, size)],
            dst_ref=recv_b.at[me, pl.ds(start, size)],
            send_sem=send_b_sem.at[g, s],
            recv_sem=recv_b_sem.at[g, me],
            device_id={"sub": s},
            device_id_type=MESH,
        )

    def send_group(g):
        def row(j, xs):
            h = lax.div(j + 1, 2)
            dz = 4 + h * (1 - 2 * lax.rem(j, 2))
            z = lax.rem(mz + dz, N_Z)
            for dx in xs:
                remote(g, lax.rem(mx + dx, N_X) * N_Z + z).start()

        def step(j, c):
            row(j, range(N_X))
            return c

        lax.fori_loop(0, N_Z - 1, step, 0)
        row(N_Z - 1, range(1, N_X))
        start, size = GROUPS[g]
        pltpu.make_async_copy(
            send_b.at[me, pl.ds(start, size)],
            recv_b.at[me, pl.ds(start, size)],
            recv_b_sem.at[g, me],
        ).start()

    for s in range(N_SUB):
        send_b[s, 0] = recv_a[TILES_I + s]
        for l in range(LEVELS):
            send_b[s, 1 + l] = recv_a[TILES_I + ancestors[l, s]]
    send_group(0)
    offset = jnp.int32(0)
    my_off = jnp.int32(0)
    for s in range(N_SUB):
        send_b[s, SEPS:] = recv_a[pl.ds(offset >> 7, WIN)]
        my_off = my_off + jnp.where(s < me, counts[s], 0)
        offset = offset + counts[s]
    for g in range(1, len(GROUPS)):
        send_group(g)
    my_count = counts[me]
    shift = my_off & 127

    def drain_a(i, c):
        copy_a(lax.rem(mv + i, N_VEC)).wait_send()
        return c

    def drain(g):
        def step(i, c):
            remote(g, lax.rem(me + i, N_SUB)).wait_send()
            return c

        lax.fori_loop(1, N_SUB, step, 0)

    def gather(g):
        start, size = GROUPS[g]

        def step(k, c):
            for q in range(4):
                s = k * 4 + q
                block = recv_b.at[s, pl.ds(start, size)]
                pltpu.make_async_copy(block, block, recv_b_sem.at[g, s]).wait()
                for t in range(start, start + size):
                    lanes[k, ROWS * q : ROWS * (q + 1), t * 128 : (t + 1) * 128] = recv_b[s, t]
            return c

        lax.fori_loop(0, N_SUB // 4, step, 0)

    lax.fori_loop(1, N_VEC, drain_a, 0)
    load_coupling.wait()

    def mask(b, c):
        rows = pl.ds(pl.multiple_of(b * BW, BW), BW)
        for l in range(LEVELS):
            cols = slice(l * BW, (l + 1) * BW)
            gate = gates[l, 0, b].astype(F32).astype(BF16)
            coupling[rows, cols] = coupling[rows, cols] * gate
        return c

    lax.fori_loop(0, NBLK, mask, 0)
    load_sep.wait()
    load_modes.wait()
    gather(0)

    def field_of(index, t):
        block = lanes[:, :, t * 128 : (t + 1) * 128].reshape(128, 128)
        return lax.dot_general(sep[index], block, NT, preferred_element_type=F32).astype(BF16)

    field[...] = field_of(me, 0)
    for l in range(LEVELS):
        above[l * BW : (l + 1) * BW, :] = field_of(ancestors[l, me], 1 + l)

    def couple(b, c):
        rows = pl.ds(pl.multiple_of(b * 512, 512), 512)
        total[rows, :] = jnp.dot(coupling[rows, :], above[...], preferred_element_type=F32)
        return c

    lax.fori_loop(0, PHYS // 512, couple, 0)
    row = lax.broadcasted_iota(jnp.int32, (128, 256), 0)
    col = lax.broadcasted_iota(jnp.int32, (128, 256), 1)

    def interior(g):
        first, count = CHUNKS[g]
        gather(g + 1)
        for t in range(first, first + count):
            pick = jnp.where((col == row + shift) & (row + t * 128 < my_count), 1.0, 0.0)
            pair = lanes[:, :, (SEPS + t) * 128 : (SEPS + t + 2) * 128].reshape(128, 256)
            weights[t * 128 : (t + 1) * 128, :] = lax.dot_general(
                pick.astype(BF16), pair, NT, preferred_element_type=F32
            ).astype(BF16)
        cols = slice(first * 128, (first + count) * 128)

        def step(b, c):
            rows = pl.ds(pl.multiple_of(b * 512, 512), 512)
            part = total[rows, :] + jnp.dot(
                modes[rows, cols], weights[cols, :], preferred_element_type=F32
            )
            if g < len(CHUNKS) - 1:
                total[rows, :] = part
            else:
                out[rows, :] = part.astype(BF16)
            return c

        lax.fori_loop(0, PHYS // 512, step, 0)

    interior(0)
    interior(1)
    for g in range(len(GROUPS) - 1):
        drain(g)
    interior(2)
    drain(len(GROUPS) - 1)


def body(coefficients, row_counts, ancestors, interior_modes, separator_modes, coupling, pattern):
    hbm = pl.BlockSpec(memory_space=pl.ANY)
    vmem = pl.BlockSpec(memory_space=pltpu.VMEM)
    dma = pltpu.SemaphoreType.DMA
    return pl.pallas_call(
        kernel,
        out_shape=(pltpu.VMEM((PHYS, 128), BF16), pltpu.VMEM((BW, 128), BF16)),
        in_specs=[hbm] * 7,
        out_specs=(vmem, vmem),
        scratch_shapes=[
            pltpu.SMEM((N_SUB,), jnp.int32),
            pltpu.SMEM((LEVELS, N_SUB), jnp.int32),
            pltpu.SMEM((LEVELS, 1, NBLK), jnp.int32),
            pltpu.VMEM((ROWS * N_VEC, TILES_A * 128), BF16),
            pltpu.VMEM((PHYS, CAP), BF16),
            pltpu.VMEM((N_SUB, BW, SEPM), BF16),
            pltpu.VMEM((PHYS, LEVELS * BW), BF16),
            pltpu.VMEM((N_VEC, TILES_A, ROWS, 128), BF16),
            pltpu.VMEM((N_VEC * TILES_A, ROWS, 128), BF16),
            pltpu.VMEM((N_SUB, SLOT, ROWS, 128), BF16),
            pltpu.VMEM((N_SUB, SLOT, ROWS, 128), BF16),
            pltpu.VMEM((N_SUB // 4, 4 * ROWS, SLOT * 128), BF16),
            pltpu.VMEM((LEVELS * BW, 128), BF16),
            pltpu.VMEM((PHYS, 128), F32),
            pltpu.VMEM((CAP, 128), BF16),
            dma((7,)),
            dma((N_VEC,)),
            dma((N_VEC,)),
            dma((len(GROUPS), N_SUB)),
            dma((len(GROUPS), N_SUB)),
            pltpu.SemaphoreType.REGULAR((10,)),
        ],
        compiler_params=pltpu.CompilerParams(
            collective_id=0, has_side_effects=True, vmem_limit_bytes=60 * 1024 * 1024
        ),
        name="recover",
    )(
        row_counts,
        ancestors.T,
        jnp.transpose(pattern, (2, 0, 1)),
        coefficients,
        interior_modes,
        separator_modes.reshape(N_SUB, BW, SEPM),
        coupling,
    )


def solution(mesh):
    placed = (P("sub", "vec"), P(), P(), P("sub", None), P(), P("sub", None), P("sub", None, None))
    return jax.shard_map(
        body,
        mesh=mesh,
        in_specs=placed,
        out_specs=(P("sub", "vec"), P("sub", "vec")),
        check_vma=False,
    )
```

```python
import jax
import jax.numpy as jnp
from jax import lax
from jax.experimental import pallas as pl
from jax.experimental.pallas import tpu as pltpu
from jax.sharding import PartitionSpec as P

BW = 256
SEPM = 128
LEVELS = 3
N_SUB = 32
N_X = 4
N_Z = 8
N_VEC = 8
ROWS = 4
TILES_A = 20
TILES_I = 128
SEPS = 1 + LEVELS
WIN = 9
GROUPS = ((0, WIN, 0, 8),)
CAP = 1024
PHYS = 4096
NBLK = PHYS // BW
MESH = pl.DeviceIdType.MESH
BF16 = jnp.bfloat16
F32 = jnp.float32
NT = (((1,), (1,)), ((), ()))


def kernel(
    counts_hbm,
    ancestors_hbm,
    gates_hbm,
    coef_hbm,
    modes_hbm,
    sep_hbm,
    coupling_hbm,
    out,
    field,
    counts,
    ancestors,
    gates,
    coef,
    modes,
    sep,
    coupling,
    send_a,
    recv_i,
    recv_s,
    lanes,
    above,
    total,
    weights,
    load_sem,
    send_a_sem,
    recv_a_sem,
    send_b_sem,
    recv_b_sem,
    relay_sem,
    *slots,
):
    send_b = slots[: len(slots) // 2]
    recv_b = slots[len(slots) // 2 :]
    me = lax.axis_index("sub")
    mv = lax.axis_index("vec")
    mx = lax.div(me, N_Z)
    mz = lax.rem(me, N_Z)

    def along_z(d):
        return mx * N_Z + lax.rem(mz + N_Z + d, N_Z)

    def along_x(d):
        return lax.rem(mx + N_X + d, N_X) * N_Z + mz

    def load(src, dst, i):
        return pltpu.make_async_copy(src, dst, load_sem.at[i])

    load_coef = load(coef_hbm, coef, 0)
    load_sep = load(sep_hbm, sep, 1)
    load_coupling = load(coupling_hbm, coupling, 2)
    load_modes = load(modes_hbm, modes, 3)
    load_counts = load(counts_hbm, counts, 4)
    load_ancestors = load(ancestors_hbm, ancestors, 5)
    load_gates = load(gates_hbm, gates, 6)

    barrier = pltpu.get_barrier_semaphore()
    for i in range(1, N_VEC):
        pl.semaphore_signal(
            barrier, inc=1, device_id={"vec": lax.rem(mv + i, N_VEC)}, device_id_type=MESH
        )
    near = [along_z(d) for d in (1, -1, 2, -2)] + [along_x(d) for d in (1, -1, 2)]
    for s in near:
        pl.semaphore_signal(barrier, inc=1, device_id={"sub": s}, device_id_type=MESH)
    load_coef.start()
    load_counts.start()
    load_ancestors.start()
    load_gates.start()
    load_sep.start()
    load_coupling.start()
    load_modes.start()
    load_coef.wait()

    def split_rows(t, c):
        cols = pl.ds(pl.multiple_of(t * 128, 128), 128)
        for v in range(N_VEC):
            send_a[v, t] = coef[ROWS * v : ROWS * (v + 1), cols]
        return c

    lax.fori_loop(0, TILES_A, split_rows, 0)
    recv_i[TILES_I:] = jnp.zeros((WIN - 1, ROWS, 128), BF16)
    pl.semaphore_wait(barrier, N_VEC - 1 + len(near))

    def tell(i, s):
        pl.semaphore_signal(relay_sem.at[i], inc=1, device_id={"sub": s}, device_id_type=MESH)

    tell(0, along_z(2))
    tell(1, along_z(-2))

    def send_rows(group, start, size):
        def own(v):
            return send_a.at[v, pl.ds(start, size)]

        there = (recv_s, recv_i)[group].at[
            pl.ds(mv * TILES_A + start - (0 if group else TILES_I), size)
        ]

        def step(i, c):
            v = lax.rem(mv + i, N_VEC)
            pltpu.make_async_remote_copy(
                src_ref=own(v),
                dst_ref=there,
                send_sem=send_a_sem.at[0],
                recv_sem=recv_a_sem.at[group],
                device_id={"vec": v},
                device_id_type=MESH,
            ).start()
            return c

        lax.fori_loop(1, N_VEC, step, 0)
        pltpu.make_async_copy(own(mv), there, recv_a_sem.at[group]).start()

    split = TILES_I // TILES_A
    cut = TILES_I - split * TILES_A

    @pl.when(mv < split)
    def _():
        send_rows(1, 0, TILES_A)

    @pl.when(mv == split)
    def _():
        send_rows(0, cut, TILES_A - cut)
        send_rows(1, 0, cut)

    @pl.when(mv > split)
    def _():
        send_rows(0, 0, TILES_A)

    def settle(ref, sem):
        pltpu.make_async_copy(ref, ref, sem).wait()

    load_counts.wait()
    load_ancestors.wait()
    load_gates.wait()
    pl.semaphore_wait(relay_sem.at[0], 1)
    pl.semaphore_wait(relay_sem.at[1], 1)
    tell(2, along_x(1))
    tell(3, along_x(-1))
    tell(4, along_x(2))
    pl.semaphore_wait(relay_sem.at[2], 1)
    pl.semaphore_wait(relay_sem.at[3], 1)
    pl.semaphore_wait(relay_sem.at[4], 1)

    def send_group(g):
        def row(j, xs):
            h = lax.div(j + 1, 2)
            dz = 4 + h * (1 - 2 * lax.rem(j, 2))
            z = lax.rem(mz + dz, N_Z)
            for dx in xs:
                s = lax.rem(mx + dx, N_X) * N_Z + z
                pltpu.make_async_remote_copy(
                    src_ref=send_b[g].at[s],
                    dst_ref=recv_b[g].at[me],
                    send_sem=send_b_sem.at[g],
                    recv_sem=recv_b_sem.at[g],
                    device_id={"sub": s},
                    device_id_type=MESH,
                ).start()

        def step(j, c):
            row(j, range(N_X))
            return c

        lax.fori_loop(0, N_Z - 1, step, 0)
        row(N_Z - 1, range(1, N_X))
        pltpu.make_async_copy(send_b[g].at[me], recv_b[g].at[me], recv_b_sem.at[g]).start()

    settle(recv_s, recv_a_sem.at[0])
    for s in range(N_SUB):
        send_b[0][s, 0] = recv_s[s]
        for l in range(LEVELS):
            send_b[0][s, 1 + l] = recv_s[ancestors[l, s]]
    send_group(0)
    settle(recv_i.at[pl.ds(0, TILES_I)], recv_a_sem.at[1])
    offset = jnp.int32(0)
    my_off = jnp.int32(0)
    for s in range(N_SUB):
        for g, (start, size, _, _) in enumerate(GROUPS):
            send_b[1 + g][s] = recv_i[pl.ds((offset >> 7) + start, size)]
        my_off = my_off + jnp.where(s < me, counts[s], 0)
        offset = offset + counts[s]
    for g in range(len(GROUPS)):
        send_group(1 + g)
    my_count = counts[me]
    shift = my_off & 127

    def gather(g, start, size):
        settle(recv_b[g], recv_b_sem.at[g])

        def step(k, c):
            for q in range(4):
                for t in range(size):
                    cols = slice((start + t) * 128, (start + t + 1) * 128)
                    lanes[k, ROWS * q : ROWS * (q + 1), cols] = recv_b[g][k * 4 + q, t]
            return c

        lax.fori_loop(0, N_SUB // 4, step, 0)

    load_coupling.wait()

    def mask(b, c):
        rows = pl.ds(pl.multiple_of(b * BW, BW), BW)
        for l in range(LEVELS):
            cols = slice(l * BW, (l + 1) * BW)
            gate = gates[l, 0, b].astype(F32).astype(BF16)
            coupling[rows, cols] = coupling[rows, cols] * gate
        return c

    lax.fori_loop(0, NBLK, mask, 0)
    load_sep.wait()
    load_modes.wait()
    settle(send_a.at[pl.ds(0, N_VEC - 1)], send_a_sem.at[0])
    gather(0, 0, SEPS)

    def field_of(index, t):
        block = lanes[:, :, t * 128 : (t + 1) * 128].reshape(128, 128)
        return lax.dot_general(sep[index], block, NT, preferred_element_type=F32).astype(BF16)

    field[...] = field_of(me, 0)
    for l in range(LEVELS):
        above[l * BW : (l + 1) * BW, :] = field_of(ancestors[l, me], 1 + l)
    total[...] = jnp.dot(coupling[...], above[...], preferred_element_type=F32)
    row = lax.broadcasted_iota(jnp.int32, (128, 256), 0)
    col = lax.broadcasted_iota(jnp.int32, (128, 256), 1)
    for g, (start, size, first, last) in enumerate(GROUPS):
        gather(1 + g, SEPS + start, size)
        for t in range(first, last):
            pick = jnp.where((col == row + shift) & (row + t * 128 < my_count), 1.0, 0.0)
            pair = lanes[:, :, (SEPS + t) * 128 : (SEPS + t + 2) * 128].reshape(128, 256)
            weights[t * 128 : (t + 1) * 128, :] = lax.dot_general(
                pick.astype(BF16), pair, NT, preferred_element_type=F32
            ).astype(BF16)
        if g == len(GROUPS) - 1:
            for r in range(1 + len(GROUPS)):
                settle(send_b[r].at[pl.ds(0, N_SUB - 1)], send_b_sem.at[r])
        cols = slice(first * 128, last * 128)
        part = total[...] + jnp.dot(
            modes[:, cols], weights[cols, :], preferred_element_type=F32
        )
        if g < len(GROUPS) - 1:
            total[...] = part
        else:
            out[...] = part.astype(BF16)


def store(interior, field, interior_out, field_out, sem):
    copies = (
        pltpu.make_async_copy(interior, interior_out, sem.at[0]),
        pltpu.make_async_copy(field, field_out, sem.at[1]),
    )
    for copy in copies:
        copy.start()
    for copy in copies:
        copy.wait()


def body(coefficients, row_counts, ancestors, interior_modes, separator_modes, coupling, pattern):
    hbm = pl.BlockSpec(memory_space=pl.ANY)
    vmem = pl.BlockSpec(memory_space=pltpu.VMEM)
    dma = pltpu.SemaphoreType.DMA
    sizes = [SEPS] + [size for _, size, _, _ in GROUPS]
    slots = [pltpu.VMEM((N_SUB, size, ROWS, 128), BF16) for size in sizes]
    results = pl.pallas_call(
        kernel,
        out_shape=(pltpu.VMEM((PHYS, 128), BF16), pltpu.VMEM((BW, 128), BF16)),
        in_specs=[hbm] * 7,
        out_specs=(vmem, vmem),
        scratch_shapes=[
            pltpu.SMEM((N_SUB,), jnp.int32),
            pltpu.SMEM((LEVELS, N_SUB), jnp.int32),
            pltpu.SMEM((LEVELS, 1, NBLK), jnp.int32),
            pltpu.VMEM((ROWS * N_VEC, TILES_A * 128), BF16),
            pltpu.VMEM((PHYS, CAP), BF16),
            pltpu.VMEM((N_SUB, BW, SEPM), BF16),
            pltpu.VMEM((PHYS, LEVELS * BW), BF16),
            pltpu.VMEM((N_VEC, TILES_A, ROWS, 128), BF16),
            pltpu.VMEM((TILES_I + WIN - 1, ROWS, 128), BF16),
            pltpu.VMEM((N_SUB, ROWS, 128), BF16),
            pltpu.VMEM((N_SUB // 4, 4 * ROWS, (SEPS + WIN) * 128), BF16),
            pltpu.VMEM((LEVELS * BW, 128), BF16),
            pltpu.VMEM((PHYS, 128), F32),
            pltpu.VMEM((CAP, 128), BF16),
            dma((7,)),
            dma((1,)),
            dma((2,)),
            dma((len(sizes),)),
            dma((len(sizes),)),
            pltpu.SemaphoreType.REGULAR((5,)),
            *slots,
            *slots,
        ],
        compiler_params=pltpu.CompilerParams(
            collective_id=0, has_side_effects=True, vmem_limit_bytes=60 * 1024 * 1024
        ),
        name="recover",
    )(
        row_counts,
        ancestors.T,
        jnp.transpose(pattern, (2, 0, 1)),
        coefficients,
        interior_modes,
        separator_modes.reshape(N_SUB, BW, SEPM),
        coupling,
    )
    return pl.pallas_call(
        store,
        out_shape=tuple(jax.ShapeDtypeStruct((rows, 128), BF16) for rows in (PHYS, BW)),
        in_specs=[vmem] * 2,
        out_specs=(hbm, hbm),
        scratch_shapes=[dma((2,))],
        compiler_params=pltpu.CompilerParams(vmem_limit_bytes=8 * 1024 * 1024),
        name="store",
    )(*[pltpu.with_memory_space_constraint(x, pltpu.VMEM) for x in results])


def solution(mesh):
    placed = (P("sub", "vec"), P(), P(), P("sub", None), P(), P("sub", None), P("sub", None, None))
    return jax.shard_map(
        body,
        mesh=mesh,
        in_specs=placed,
        out_specs=(P("sub", "vec"), P("sub", "vec")),
        check_vma=False,
    )
```

```python
import jax
import jax.numpy as jnp
from jax import lax
from jax.experimental import pallas as pl
from jax.experimental.pallas import tpu as pltpu
from jax.sharding import PartitionSpec as P

BW = 256
SEPM = 128
LEVELS = 3
N_SUB = 32
N_X = 4
N_Z = 8
N_VEC = 8
ROWS = 4
TILES_A = 20
TILES_I = 128
SEPS = 1 + LEVELS
WIN = 9
GROUPS = ((0, 5, 0, 4), (5, 4, 4, 8))
CAP = 1024
PHYS = 4096
NBLK = PHYS // BW
STEP = 2048
MESH = pl.DeviceIdType.MESH
BF16 = jnp.bfloat16
F32 = jnp.float32
NT = (((1,), (1,)), ((), ()))


def kernel(
    counts_hbm,
    ancestors_hbm,
    gates_hbm,
    coef_hbm,
    modes_hbm,
    sep_hbm,
    coupling_hbm,
    out,
    field,
    counts,
    ancestors,
    gates,
    coef,
    modes,
    sep,
    coupling,
    send_a,
    recv_i,
    recv_s,
    lanes,
    above,
    total,
    weights,
    load_sem,
    send_a_sem,
    recv_a_sem,
    send_b_sem,
    recv_b_sem,
    relay_sem,
    *slots,
):
    send_b = slots[: len(slots) // 2]
    recv_b = slots[len(slots) // 2 :]
    me = lax.axis_index("sub")
    mv = lax.axis_index("vec")
    mx = lax.div(me, N_Z)
    mz = lax.rem(me, N_Z)

    def along_z(d):
        return mx * N_Z + lax.rem(mz + N_Z + d, N_Z)

    def along_x(d):
        return lax.rem(mx + N_X + d, N_X) * N_Z + mz

    def load(src, dst, i):
        return pltpu.make_async_copy(src, dst, load_sem.at[i])

    load_coef = load(coef_hbm, coef, 0)
    load_sep = load(sep_hbm, sep, 1)
    load_coupling = load(coupling_hbm, coupling, 2)
    load_modes = load(modes_hbm, modes, 3)
    load_counts = load(counts_hbm, counts, 4)
    load_ancestors = load(ancestors_hbm, ancestors, 5)
    load_gates = load(gates_hbm, gates, 6)

    barrier = pltpu.get_barrier_semaphore()
    for i in range(1, N_VEC):
        pl.semaphore_signal(
            barrier, inc=1, device_id={"vec": lax.rem(mv + i, N_VEC)}, device_id_type=MESH
        )
    near = [along_z(d) for d in (1, -1, 2, -2)] + [along_x(d) for d in (1, -1, 2)]
    for s in near:
        pl.semaphore_signal(barrier, inc=1, device_id={"sub": s}, device_id_type=MESH)
    load_coef.start()
    load_counts.start()
    load_ancestors.start()
    load_gates.start()
    load_sep.start()
    load_coupling.start()
    load_modes.start()
    load_coef.wait()

    def split_rows(t, c):
        cols = pl.ds(pl.multiple_of(t * 128, 128), 128)
        for v in range(N_VEC):
            send_a[v, t] = coef[ROWS * v : ROWS * (v + 1), cols]
        return c

    lax.fori_loop(0, TILES_A, split_rows, 0)
    recv_i[TILES_I:] = jnp.zeros((WIN - 1, ROWS, 128), BF16)
    pl.semaphore_wait(barrier, N_VEC - 1 + len(near))

    def tell(i, s):
        pl.semaphore_signal(relay_sem.at[i], inc=1, device_id={"sub": s}, device_id_type=MESH)

    tell(0, along_z(2))
    tell(1, along_z(-2))

    def send_rows(group, start, size):
        def own(v):
            return send_a.at[v, pl.ds(start, size)]

        there = (recv_s, recv_i)[group].at[
            pl.ds(mv * TILES_A + start - (0 if group else TILES_I), size)
        ]

        def step(i, c):
            v = lax.rem(mv + i, N_VEC)
            pltpu.make_async_remote_copy(
                src_ref=own(v),
                dst_ref=there,
                send_sem=send_a_sem.at[0],
                recv_sem=recv_a_sem.at[group],
                device_id={"vec": v},
                device_id_type=MESH,
            ).start()
            return c

        lax.fori_loop(1, N_VEC, step, 0)
        pltpu.make_async_copy(own(mv), there, recv_a_sem.at[group]).start()

    split = TILES_I // TILES_A
    cut = TILES_I - split * TILES_A

    @pl.when(mv < split)
    def _():
        send_rows(1, 0, TILES_A)

    @pl.when(mv == split)
    def _():
        send_rows(0, cut, TILES_A - cut)
        send_rows(1, 0, cut)

    @pl.when(mv > split)
    def _():
        send_rows(0, 0, TILES_A)

    def settle(ref, sem):
        pltpu.make_async_copy(ref, ref, sem).wait()

    load_counts.wait()
    load_ancestors.wait()
    load_gates.wait()
    pl.semaphore_wait(relay_sem.at[0], 1)
    pl.semaphore_wait(relay_sem.at[1], 1)
    tell(2, along_x(1))
    tell(3, along_x(-1))
    tell(4, along_x(2))
    pl.semaphore_wait(relay_sem.at[2], 1)
    pl.semaphore_wait(relay_sem.at[3], 1)
    pl.semaphore_wait(relay_sem.at[4], 1)

    def send_group(g):
        def row(j, xs):
            h = lax.div(j + 1, 2)
            dz = 4 + h * (1 - 2 * lax.rem(j, 2))
            z = lax.rem(mz + dz, N_Z)
            for dx in xs:
                s = lax.rem(mx + dx, N_X) * N_Z + z
                pltpu.make_async_remote_copy(
                    src_ref=send_b[g].at[s],
                    dst_ref=recv_b[g].at[me],
                    send_sem=send_b_sem.at[g],
                    recv_sem=recv_b_sem.at[g],
                    device_id={"sub": s},
                    device_id_type=MESH,
                ).start()

        def step(j, c):
            row(j, range(N_X))
            return c

        lax.fori_loop(0, N_Z - 1, step, 0)
        row(N_Z - 1, range(1, N_X))
        pltpu.make_async_copy(send_b[g].at[me], recv_b[g].at[me], recv_b_sem.at[g]).start()

    settle(recv_s, recv_a_sem.at[0])
    for s in range(N_SUB):
        send_b[0][s, 0] = recv_s[s]
        for l in range(LEVELS):
            send_b[0][s, 1 + l] = recv_s[ancestors[l, s]]
    send_group(0)
    settle(recv_i.at[pl.ds(0, TILES_I)], recv_a_sem.at[1])
    offset = jnp.int32(0)
    my_off = jnp.int32(0)
    for s in range(N_SUB):
        for g, (start, size, _, _) in enumerate(GROUPS):
            send_b[1 + g][s] = recv_i[pl.ds((offset >> 7) + start, size)]
        my_off = my_off + jnp.where(s < me, counts[s], 0)
        offset = offset + counts[s]
    for g in range(len(GROUPS)):
        send_group(1 + g)
    my_count = counts[me]
    shift = my_off & 127

    def gather(g, start, size):
        settle(recv_b[g], recv_b_sem.at[g])

        def step(k, c):
            for q in range(4):
                for t in range(size):
                    cols = slice((start + t) * 128, (start + t + 1) * 128)
                    lanes[k, ROWS * q : ROWS * (q + 1), cols] = recv_b[g][k * 4 + q, t]
            return c

        lax.fori_loop(0, N_SUB // 4, step, 0)

    load_coupling.wait()

    def mask(b, c):
        rows = pl.ds(pl.multiple_of(b * BW, BW), BW)
        for l in range(LEVELS):
            cols = slice(l * BW, (l + 1) * BW)
            gate = gates[l, 0, b].astype(F32).astype(BF16)
            coupling[rows, cols] = coupling[rows, cols] * gate
        return c

    lax.fori_loop(0, NBLK, mask, 0)
    load_sep.wait()
    load_modes.wait()
    settle(send_a.at[pl.ds(0, N_VEC - 1)], send_a_sem.at[0])
    gather(0, 0, SEPS)

    def field_of(index, t):
        block = lanes[:, :, t * 128 : (t + 1) * 128].reshape(128, 128)
        return lax.dot_general(sep[index], block, NT, preferred_element_type=F32).astype(BF16)

    field[...] = field_of(me, 0)
    for l in range(LEVELS):
        above[l * BW : (l + 1) * BW, :] = field_of(ancestors[l, me], 1 + l)

    def couple(b, c):
        rows = pl.ds(pl.multiple_of(b * STEP, STEP), STEP)
        total[rows, :] = jnp.dot(coupling[rows, :], above[...], preferred_element_type=F32)
        return c

    lax.fori_loop(0, PHYS // STEP, couple, 0)
    row = lax.broadcasted_iota(jnp.int32, (128, 256), 0)
    col = lax.broadcasted_iota(jnp.int32, (128, 256), 1)
    for g, (start, size, first, last) in enumerate(GROUPS):
        gather(1 + g, SEPS + start, size)
        for t in range(first, last):
            pick = jnp.where((col == row + shift) & (row + t * 128 < my_count), 1.0, 0.0)
            pair = lanes[:, :, (SEPS + t) * 128 : (SEPS + t + 2) * 128].reshape(128, 256)
            weights[t * 128 : (t + 1) * 128, :] = lax.dot_general(
                pick.astype(BF16), pair, NT, preferred_element_type=F32
            ).astype(BF16)
        if g == len(GROUPS) - 1:
            for r in range(1 + len(GROUPS)):
                settle(send_b[r].at[pl.ds(0, N_SUB - 1)], send_b_sem.at[r])
        cols = slice(first * 128, last * 128)

        def finish(b, c):
            rows = pl.ds(pl.multiple_of(b * STEP, STEP), STEP)
            part = total[rows, :] + jnp.dot(
                modes[rows, cols], weights[cols, :], preferred_element_type=F32
            )
            if g < len(GROUPS) - 1:
                total[rows, :] = part
            else:
                out[rows, :] = part.astype(BF16)
            return c

        lax.fori_loop(0, PHYS // STEP, finish, 0)


def store(interior, field, interior_out, field_out, sem):
    copies = (
        pltpu.make_async_copy(interior, interior_out, sem.at[0]),
        pltpu.make_async_copy(field, field_out, sem.at[1]),
    )
    for copy in copies:
        copy.start()
    for copy in copies:
        copy.wait()


def body(coefficients, row_counts, ancestors, interior_modes, separator_modes, coupling, pattern):
    hbm = pl.BlockSpec(memory_space=pl.ANY)
    vmem = pl.BlockSpec(memory_space=pltpu.VMEM)
    dma = pltpu.SemaphoreType.DMA
    sizes = [SEPS] + [size for _, size, _, _ in GROUPS]
    slots = [pltpu.VMEM((N_SUB, size, ROWS, 128), BF16) for size in sizes]
    results = pl.pallas_call(
        kernel,
        out_shape=(pltpu.VMEM((PHYS, 128), BF16), pltpu.VMEM((BW, 128), BF16)),
        in_specs=[hbm] * 7,
        out_specs=(vmem, vmem),
        scratch_shapes=[
            pltpu.SMEM((N_SUB,), jnp.int32),
            pltpu.SMEM((LEVELS, N_SUB), jnp.int32),
            pltpu.SMEM((LEVELS, 1, NBLK), jnp.int32),
            pltpu.VMEM((ROWS * N_VEC, TILES_A * 128), BF16),
            pltpu.VMEM((PHYS, CAP), BF16),
            pltpu.VMEM((N_SUB, BW, SEPM), BF16),
            pltpu.VMEM((PHYS, LEVELS * BW), BF16),
            pltpu.VMEM((N_VEC, TILES_A, ROWS, 128), BF16),
            pltpu.VMEM((TILES_I + WIN - 1, ROWS, 128), BF16),
            pltpu.VMEM((N_SUB, ROWS, 128), BF16),
            pltpu.VMEM((N_SUB // 4, 4 * ROWS, (SEPS + WIN) * 128), BF16),
            pltpu.VMEM((LEVELS * BW, 128), BF16),
            pltpu.VMEM((PHYS, 128), F32),
            pltpu.VMEM((CAP, 128), BF16),
            dma((7,)),
            dma((1,)),
            dma((2,)),
            dma((len(sizes),)),
            dma((len(sizes),)),
            pltpu.SemaphoreType.REGULAR((5,)),
            *slots,
            *slots,
        ],
        compiler_params=pltpu.CompilerParams(
            collective_id=0, has_side_effects=True, vmem_limit_bytes=60 * 1024 * 1024
        ),
        name="recover",
    )(
        row_counts,
        ancestors.T,
        jnp.transpose(pattern, (2, 0, 1)),
        coefficients,
        interior_modes,
        separator_modes.reshape(N_SUB, BW, SEPM),
        coupling,
    )
    return pl.pallas_call(
        store,
        out_shape=tuple(jax.ShapeDtypeStruct((rows, 128), BF16) for rows in (PHYS, BW)),
        in_specs=[vmem] * 2,
        out_specs=(hbm, hbm),
        scratch_shapes=[dma((2,))],
        compiler_params=pltpu.CompilerParams(vmem_limit_bytes=8 * 1024 * 1024),
        name="store",
    )(*[pltpu.with_memory_space_constraint(x, pltpu.VMEM) for x in results])


def solution(mesh):
    placed = (P("sub", "vec"), P(), P(), P("sub", None), P(), P("sub", None), P("sub", None, None))
    return jax.shard_map(
        body,
        mesh=mesh,
        in_specs=placed,
        out_specs=(P("sub", "vec"), P("sub", "vec")),
        check_vma=False,
    )
```

```python
import jax
import jax.numpy as jnp
from jax import lax
from jax.experimental import pallas as pl
from jax.experimental.pallas import tpu as pltpu
from jax.sharding import PartitionSpec as P

BW = 256
SEPM = 128
LEVELS = 3
N_SUB = 32
N_X = 4
N_Z = 8
N_VEC = 8
ROWS = 4
TILES_A = 20
TILES_I = 128
SEPS = LEVELS + 1
WIN = 9
GROUPS = ((0, 3), (3, 4), (7, 3), (10, 2))
LAST = 6 * 128
CAP = 1024
PHYS = 4096
NBLK = PHYS // BW
STEP = 2048
MESH = pl.DeviceIdType.MESH
BF16 = jnp.bfloat16
F32 = jnp.float32
NT = (((1,), (1,)), ((), ()))


def kernel(
    counts_hbm,
    ancestors_hbm,
    gates_hbm,
    coef_hbm,
    modes_hbm,
    sep_hbm,
    coupling_hbm,
    total,
    modes_last,
    coef_last,
    field,
    counts,
    ancestors,
    gates,
    coef,
    modes,
    sep,
    coupling,
    send_a,
    recv_i,
    recv_s,
    lanes,
    above,
    load_sem,
    send_a_sem,
    recv_a_sem,
    send_b_sem,
    recv_b_sem,
    relay_sem,
    *slots,
):
    send_b = slots[: len(slots) // 2]
    recv_b = slots[len(slots) // 2 :]
    me = lax.axis_index("sub")
    mv = lax.axis_index("vec")
    mx = lax.div(me, N_Z)
    mz = lax.rem(me, N_Z)

    def along_z(d):
        return mx * N_Z + lax.rem(mz + N_Z + d, N_Z)

    def along_x(d):
        return lax.rem(mx + N_X + d, N_X) * N_Z + mz

    def load(src, dst, i):
        return pltpu.make_async_copy(src, dst, load_sem.at[i])

    load_coef = load(coef_hbm, coef, 0)
    load_sep = load(sep_hbm, sep, 1)
    load_coupling = load(coupling_hbm, coupling, 2)
    load_modes = load(modes_hbm.at[:, pl.ds(0, LAST)], modes, 3)
    load_last = load(modes_hbm.at[:, pl.ds(LAST, CAP - LAST)], modes_last, 7)
    load_counts = load(counts_hbm, counts, 4)
    load_ancestors = load(ancestors_hbm, ancestors, 5)
    load_gates = load(gates_hbm, gates, 6)

    barrier = pltpu.get_barrier_semaphore()
    for i in range(1, N_VEC):
        pl.semaphore_signal(
            barrier, inc=1, device_id={"vec": lax.rem(mv + i, N_VEC)}, device_id_type=MESH
        )
    near = [along_z(d) for d in (1, -1, 2, -2)] + [along_x(d) for d in (1, -1, 2)]
    for s in near:
        pl.semaphore_signal(barrier, inc=1, device_id={"sub": s}, device_id_type=MESH)
    load_coef.start()
    load_counts.start()
    load_ancestors.start()
    load_gates.start()
    load_sep.start()
    load_coupling.start()
    load_modes.start()
    load_last.start()
    load_coef.wait()

    def split_rows(t, c):
        cols = pl.ds(pl.multiple_of(t * 128, 128), 128)
        for v in range(N_VEC):
            send_a[v, t] = coef[ROWS * v : ROWS * (v + 1), cols]
        return c

    lax.fori_loop(0, TILES_A, split_rows, 0)
    recv_i[TILES_I:] = jnp.zeros((WIN - 1, ROWS, 128), BF16)
    pl.semaphore_wait(barrier, N_VEC - 1 + len(near))

    def tell(i, s):
        pl.semaphore_signal(relay_sem.at[i], inc=1, device_id={"sub": s}, device_id_type=MESH)

    tell(0, along_z(2))
    tell(1, along_z(-2))

    def send_rows(group, start, size):
        def own(v):
            return send_a.at[v, pl.ds(start, size)]

        there = (recv_s, recv_i)[group].at[
            pl.ds(mv * TILES_A + start - (0 if group else TILES_I), size)
        ]

        def step(i, c):
            v = lax.rem(mv + i, N_VEC)
            pltpu.make_async_remote_copy(
                src_ref=own(v),
                dst_ref=there,
                send_sem=send_a_sem.at[0],
                recv_sem=recv_a_sem.at[group],
                device_id={"vec": v},
                device_id_type=MESH,
            ).start()
            return c

        lax.fori_loop(1, N_VEC, step, 0)
        pltpu.make_async_copy(own(mv), there, recv_a_sem.at[group]).start()

    split = TILES_I // TILES_A
    cut = TILES_I - split * TILES_A

    @pl.when(mv < split)
    def _():
        send_rows(1, 0, TILES_A)

    @pl.when(mv == split)
    def _():
        send_rows(0, cut, TILES_A - cut)
        send_rows(1, 0, cut)

    @pl.when(mv > split)
    def _():
        send_rows(0, 0, TILES_A)

    def settle(ref, sem):
        pltpu.make_async_copy(ref, ref, sem).wait()

    load_counts.wait()
    load_ancestors.wait()
    load_gates.wait()
    pl.semaphore_wait(relay_sem.at[0], 1)
    pl.semaphore_wait(relay_sem.at[1], 1)
    tell(2, along_x(1))
    tell(3, along_x(-1))
    tell(4, along_x(2))
    pl.semaphore_wait(relay_sem.at[2], 1)
    pl.semaphore_wait(relay_sem.at[3], 1)
    pl.semaphore_wait(relay_sem.at[4], 1)

    def send_group(g):
        def row(j, xs):
            h = lax.div(j + 1, 2)
            dz = 4 + h * (1 - 2 * lax.rem(j, 2))
            z = lax.rem(mz + dz, N_Z)
            for dx in xs:
                s = lax.rem(mx + dx, N_X) * N_Z + z
                pltpu.make_async_remote_copy(
                    src_ref=send_b[g].at[s],
                    dst_ref=recv_b[g].at[me],
                    send_sem=send_b_sem.at[g],
                    recv_sem=recv_b_sem.at[g],
                    device_id={"sub": s},
                    device_id_type=MESH,
                ).start()

        def step(j, c):
            row(j, range(N_X))
            return c

        lax.fori_loop(0, N_Z - 1, step, 0)
        row(N_Z - 1, range(1, N_X))
        pltpu.make_async_copy(send_b[g].at[me], recv_b[g].at[me], recv_b_sem.at[g]).start()

    settle(recv_s, recv_a_sem.at[0])
    for s in range(N_SUB):
        send_b[1][s, 0] = recv_s[s]
        for l in range(LEVELS):
            send_b[0][s, l] = recv_s[ancestors[l, s]]
    send_group(0)
    settle(recv_i.at[pl.ds(0, TILES_I)], recv_a_sem.at[1])
    offset = jnp.int32(0)
    starts = []
    for s in range(N_SUB):
        starts.append(offset)
        offset = offset + counts[s]
    for g in range(1, len(GROUPS)):
        skip = 1 if g == 1 else 0
        first = GROUPS[g][0] + skip - SEPS
        size = GROUPS[g][1] - skip
        lane = lax.broadcasted_iota(jnp.int32, (size, ROWS, 128), 2)
        place = lane + 128 * (first + lax.broadcasted_iota(jnp.int32, (size, ROWS, 128), 0))
        for s in range(N_SUB):
            shift = starts[s] & 127
            tiles = recv_i[pl.ds((starts[s] >> 7) + first, size + 1)].astype(F32)
            turned = pltpu.roll(tiles, (128 - shift) & 127, 2)
            window = jnp.where(lane < 128 - shift, turned[:size], turned[1:])
            window = jnp.where(place < counts[s], window, 0.0)
            send_b[g][s, skip:] = window.astype(BF16)
        send_group(g)

    def gather(g):
        start, size = GROUPS[g]
        settle(recv_b[g], recv_b_sem.at[g])

        def step(k, c):
            for q in range(4):
                for t in range(size):
                    cols = slice((start + t) * 128, (start + t + 1) * 128)
                    lanes[k, ROWS * q : ROWS * (q + 1), cols] = recv_b[g][k * 4 + q, t]
            return c

        lax.fori_loop(0, N_SUB // 4, step, 0)

    load_coupling.wait()

    def mask(b, c):
        rows = pl.ds(pl.multiple_of(b * BW, BW), BW)
        for l in range(LEVELS):
            cols = slice(l * BW, (l + 1) * BW)
            gate = gates[l, 0, b].astype(F32).astype(BF16)
            coupling[rows, cols] = coupling[rows, cols] * gate
        return c

    lax.fori_loop(0, NBLK, mask, 0)
    load_sep.wait()
    load_modes.wait()
    load_last.wait()
    settle(send_a.at[pl.ds(0, N_VEC - 1)], send_a_sem.at[0])
    gather(0)

    def field_of(index, t):
        block = lanes[:, :, t * 128 : (t + 1) * 128].reshape(128, 128)
        return lax.dot_general(sep[index], block, NT, preferred_element_type=F32).astype(BF16)

    for l in range(LEVELS):
        above[l * BW : (l + 1) * BW, :] = field_of(ancestors[l, me], l)

    def couple(b, c):
        rows = pl.ds(pl.multiple_of(b * STEP, STEP), STEP)
        total[rows, :] = jnp.dot(coupling[rows, :], above[...], preferred_element_type=F32)
        return c

    lax.fori_loop(0, PHYS // STEP, couple, 0)
    for g in range(1, len(GROUPS) - 1):
        gather(g)
        first, size = GROUPS[g]
        if g == 1:
            field[...] = field_of(me, LEVELS)
            first, size = first + 1, size - 1
        wide = slice(first * 128, (first + size) * 128)
        cols = slice((first - SEPS) * 128, (first - SEPS + size) * 128)

        def add(b, c):
            rows = pl.ds(pl.multiple_of(b * STEP, STEP), STEP)
            total[rows, :] = total[rows, :] + lax.dot_general(
                modes[rows, cols],
                lanes[:, :, wide].reshape(128, wide.stop - wide.start),
                NT,
                preferred_element_type=F32,
            )
            return c

        lax.fori_loop(0, PHYS // STEP, add, 0)
    gather(len(GROUPS) - 1)
    coef_last[...] = lanes[:, :, SEPS * 128 + LAST :].reshape(128, CAP - LAST)
    for g in range(len(GROUPS)):
        settle(send_b[g].at[pl.ds(0, N_SUB - 1)], send_b_sem.at[g])


def finish(total, modes, coef, field, interior_out, field_out, interior, sem, field_sem):
    store_field = pltpu.make_async_copy(field, field_out, field_sem.at[0])
    store_field.start()

    def rows_of(b):
        return pl.ds(pl.multiple_of(b * STEP, STEP), STEP)

    def store(b):
        return pltpu.make_async_copy(
            interior.at[rows_of(b)], interior_out.at[rows_of(b)], sem.at[b]
        )

    def step(b, c):
        rows = rows_of(b)
        part = total[rows, :] + lax.dot_general(
            modes[rows, :], coef[...], NT, preferred_element_type=F32
        )
        interior[rows, :] = part.astype(BF16)
        store(b).start()
        return c

    lax.fori_loop(0, PHYS // STEP, step, 0)
    store_field.wait()
    for b in range(PHYS // STEP):
        store(b).wait()


def body(coefficients, row_counts, ancestors, interior_modes, separator_modes, coupling, pattern):
    hbm = pl.BlockSpec(memory_space=pl.ANY)
    vmem = pl.BlockSpec(memory_space=pltpu.VMEM)
    dma = pltpu.SemaphoreType.DMA
    sizes = [size for _, size in GROUPS]
    slots = [pltpu.VMEM((N_SUB, size, ROWS, 128), BF16) for size in sizes]
    results = pl.pallas_call(
        kernel,
        out_shape=(
            pltpu.VMEM((PHYS, 128), F32),
            pltpu.VMEM((PHYS, CAP - LAST), BF16),
            pltpu.VMEM((128, CAP - LAST), BF16),
            pltpu.VMEM((BW, 128), BF16),
        ),
        in_specs=[hbm] * 7,
        out_specs=(vmem,) * 4,
        scratch_shapes=[
            pltpu.SMEM((N_SUB,), jnp.int32),
            pltpu.SMEM((LEVELS, N_SUB), jnp.int32),
            pltpu.SMEM((LEVELS, 1, NBLK), jnp.int32),
            pltpu.VMEM((ROWS * N_VEC, TILES_A * 128), BF16),
            pltpu.VMEM((PHYS, LAST), BF16),
            pltpu.VMEM((N_SUB, BW, SEPM), BF16),
            pltpu.VMEM((PHYS, LEVELS * BW), BF16),
            pltpu.VMEM((N_VEC, TILES_A, ROWS, 128), BF16),
            pltpu.VMEM((TILES_I + WIN - 1, ROWS, 128), BF16),
            pltpu.VMEM((N_SUB, ROWS, 128), BF16),
            pltpu.VMEM((N_SUB // 4, 4 * ROWS, SEPS * 128 + CAP), BF16),
            pltpu.VMEM((LEVELS * BW, 128), BF16),
            dma((8,)),
            dma((1,)),
            dma((2,)),
            dma((len(sizes),)),
            dma((len(sizes),)),
            pltpu.SemaphoreType.REGULAR((5,)),
            *slots,
            *slots,
        ],
        compiler_params=pltpu.CompilerParams(
            collective_id=0, has_side_effects=True, vmem_limit_bytes=48 * 1024 * 1024
        ),
        name="recover",
    )(
        *[
            pltpu.with_memory_space_constraint(x, pltpu.HBM)
            for x in (
                row_counts,
                ancestors.T,
                jnp.transpose(pattern, (2, 0, 1)),
                coefficients,
                interior_modes,
                separator_modes.reshape(N_SUB, BW, SEPM),
                coupling,
            )
        ]
    )
    return pl.pallas_call(
        finish,
        out_shape=tuple(jax.ShapeDtypeStruct((rows, 128), BF16) for rows in (PHYS, BW)),
        in_specs=[vmem] * 4,
        out_specs=(hbm, hbm),
        scratch_shapes=[pltpu.VMEM((PHYS, 128), BF16), dma((PHYS // STEP,)), dma((1,))],
        compiler_params=pltpu.CompilerParams(vmem_limit_bytes=8 * 1024 * 1024),
        name="finish",
    )(*[pltpu.with_memory_space_constraint(x, pltpu.VMEM) for x in results])


def solution(mesh):
    placed = (P("sub", "vec"), P(), P(), P("sub", None), P(), P("sub", None), P("sub", None, None))
    return jax.shard_map(
        body,
        mesh=mesh,
        in_specs=placed,
        out_specs=(P("sub", "vec"), P("sub", "vec")),
        check_vma=False,
    )
```

```python
import jax
import jax.numpy as jnp
from jax import lax
from jax.experimental import pallas as pl
from jax.experimental.pallas import tpu as pltpu
from jax.sharding import PartitionSpec as P

BW = 256
SEPM = 128
LEVELS = 3
N_SUB = 32
N_X = 4
N_Z = 8
N_VEC = 8
ROWS = 4
TILES_A = 20
TILES_I = 128
SEPS = LEVELS + 1
WIN = 9
GROUPS = ((0, 3), (3, 4), (7, 3), (10, 2))
LAST = 6 * 128
CAP = 1024
PHYS = 4096
NBLK = PHYS // BW
STEP = 2048
MESH = pl.DeviceIdType.MESH
BF16 = jnp.bfloat16
F32 = jnp.float32
NT = (((1,), (1,)), ((), ()))


def kernel(
    counts_hbm,
    ancestors_hbm,
    gates_hbm,
    coef_hbm,
    modes_hbm,
    sep_hbm,
    coupling_hbm,
    total,
    modes_last,
    coef_last,
    field,
    counts,
    ancestors,
    gates,
    coef,
    modes,
    sep,
    coupling,
    send_a,
    recv_i,
    recv_s,
    lanes,
    above,
    load_sem,
    send_a_sem,
    recv_a_sem,
    send_b_sem,
    recv_b_sem,
    relay_sem,
    *slots,
):
    send_b = slots[: len(slots) // 2]
    recv_b = slots[len(slots) // 2 :]
    me = lax.axis_index("sub")
    mv = lax.axis_index("vec")
    mx = lax.div(me, N_Z)
    mz = lax.rem(me, N_Z)

    def along_z(d):
        return mx * N_Z + lax.rem(mz + N_Z + d, N_Z)

    def along_x(d):
        return lax.rem(mx + N_X + d, N_X) * N_Z + mz

    def load(src, dst, i):
        return pltpu.make_async_copy(src, dst, load_sem.at[i])

    load_coef = load(coef_hbm, coef, 0)
    load_sep = load(sep_hbm, sep, 1)
    load_coupling = load(coupling_hbm, coupling, 2)
    load_modes = load(modes_hbm.at[:, pl.ds(0, LAST)], modes, 3)
    load_last = load(modes_hbm.at[:, pl.ds(LAST, CAP - LAST)], modes_last, 7)
    load_counts = load(counts_hbm, counts, 4)
    load_ancestors = load(ancestors_hbm, ancestors, 5)
    load_gates = load(gates_hbm, gates, 6)

    barrier = pltpu.get_barrier_semaphore()
    for i in range(1, N_VEC):
        pl.semaphore_signal(
            barrier, inc=1, device_id={"vec": lax.rem(mv + i, N_VEC)}, device_id_type=MESH
        )
    near = [along_z(d) for d in (1, -1, 2, -2)] + [along_x(d) for d in (1, -1, 2)]
    for s in near:
        pl.semaphore_signal(barrier, inc=1, device_id={"sub": s}, device_id_type=MESH)
    load_coef.start()
    load_counts.start()
    load_ancestors.start()
    load_gates.start()
    load_sep.start()
    load_coupling.start()
    load_modes.start()
    load_last.start()
    load_coef.wait()

    def split_rows(t, c):
        cols = pl.ds(pl.multiple_of(t * 128, 128), 128)
        for v in range(N_VEC):
            send_a[v, t] = coef[ROWS * v : ROWS * (v + 1), cols]
        return c

    lax.fori_loop(0, TILES_A, split_rows, 0)
    recv_i[TILES_I:] = jnp.zeros((WIN - 1, ROWS, 128), BF16)
    pl.semaphore_wait(barrier, N_VEC - 1 + len(near))

    def tell(i, s):
        pl.semaphore_signal(relay_sem.at[i], inc=1, device_id={"sub": s}, device_id_type=MESH)

    tell(0, along_z(2))
    tell(1, along_z(-2))

    def send_rows(group, start, size):
        def own(v):
            return send_a.at[v, pl.ds(start, size)]

        there = (recv_s, recv_i)[group].at[
            pl.ds(mv * TILES_A + start - (0 if group else TILES_I), size)
        ]

        def step(i, c):
            v = lax.rem(mv + i, N_VEC)
            pltpu.make_async_remote_copy(
                src_ref=own(v),
                dst_ref=there,
                send_sem=send_a_sem.at[0],
                recv_sem=recv_a_sem.at[group],
                device_id={"vec": v},
                device_id_type=MESH,
            ).start()
            return c

        lax.fori_loop(1, N_VEC, step, 0)
        pltpu.make_async_copy(own(mv), there, recv_a_sem.at[group]).start()

    split = TILES_I // TILES_A
    cut = TILES_I - split * TILES_A

    @pl.when(mv < split)
    def _():
        send_rows(1, 0, TILES_A)

    @pl.when(mv == split)
    def _():
        send_rows(0, cut, TILES_A - cut)
        send_rows(1, 0, cut)

    @pl.when(mv > split)
    def _():
        send_rows(0, 0, TILES_A)

    def settle(ref, sem):
        pltpu.make_async_copy(ref, ref, sem).wait()

    load_counts.wait()
    load_ancestors.wait()
    load_gates.wait()
    pl.semaphore_wait(relay_sem.at[0], 1)
    pl.semaphore_wait(relay_sem.at[1], 1)
    tell(2, along_x(1))
    tell(3, along_x(-1))
    tell(4, along_x(2))
    pl.semaphore_wait(relay_sem.at[2], 1)
    pl.semaphore_wait(relay_sem.at[3], 1)
    pl.semaphore_wait(relay_sem.at[4], 1)

    def send_group(g):
        def place(j):
            h = lax.div(j + 1, 2)
            dz = (1 - 2 * lax.rem(mv, 2)) * h * (1 - 2 * lax.rem(j, 2))
            return lax.rem(mz + 12 + dz, N_Z)

        def send(z, dxs):
            for dx in dxs:
                s = lax.rem(mx + dx, N_X) * N_Z + z
                pltpu.make_async_remote_copy(
                    src_ref=send_b[g].at[s],
                    dst_ref=recv_b[g].at[me],
                    send_sem=send_b_sem.at[g],
                    recv_sem=recv_b_sem.at[g],
                    device_id={"sub": s},
                    device_id_type=MESH,
                ).start()

        def step(j, c):
            send(place(j), (2, 1, 3, 0))
            return c

        lax.fori_loop(0, 7, step, 0)
        send(mz, (2, 1, 3))
        pltpu.make_async_copy(send_b[g].at[me], recv_b[g].at[me], recv_b_sem.at[g]).start()

    settle(recv_s, recv_a_sem.at[0])
    for s in range(N_SUB):
        send_b[1][s, 0] = recv_s[s]
        for l in range(LEVELS):
            send_b[0][s, l] = recv_s[ancestors[l, s]]
    send_group(0)
    settle(recv_i.at[pl.ds(0, TILES_I)], recv_a_sem.at[1])
    offset = jnp.int32(0)
    starts = []
    for s in range(N_SUB):
        starts.append(offset)
        offset = offset + counts[s]
    for g in range(1, len(GROUPS)):
        skip = 1 if g == 1 else 0
        first = GROUPS[g][0] + skip - SEPS
        size = GROUPS[g][1] - skip
        lane = lax.broadcasted_iota(jnp.int32, (size, ROWS, 128), 2)
        place = lane + 128 * (first + lax.broadcasted_iota(jnp.int32, (size, ROWS, 128), 0))
        for s in range(N_SUB):
            shift = starts[s] & 127
            tiles = recv_i[pl.ds((starts[s] >> 7) + first, size + 1)].astype(F32)
            turned = pltpu.roll(tiles, (128 - shift) & 127, 2)
            window = jnp.where(lane < 128 - shift, turned[:size], turned[1:])
            window = jnp.where(place < counts[s], window, 0.0)
            send_b[g][s, skip:] = window.astype(BF16)
        send_group(g)

    def gather(g):
        start, size = GROUPS[g]
        settle(recv_b[g], recv_b_sem.at[g])

        def step(k, c):
            for q in range(4):
                for t in range(size):
                    cols = slice((start + t) * 128, (start + t + 1) * 128)
                    lanes[k, ROWS * q : ROWS * (q + 1), cols] = recv_b[g][k * 4 + q, t]
            return c

        lax.fori_loop(0, N_SUB // 4, step, 0)

    load_coupling.wait()

    def mask(b, c):
        rows = pl.ds(pl.multiple_of(b * BW, BW), BW)
        for l in range(LEVELS):
            cols = slice(l * BW, (l + 1) * BW)
            gate = gates[l, 0, b].astype(F32).astype(BF16)
            coupling[rows, cols] = coupling[rows, cols] * gate
        return c

    lax.fori_loop(0, NBLK, mask, 0)
    load_sep.wait()
    load_modes.wait()
    load_last.wait()
    settle(send_a.at[pl.ds(0, N_VEC - 1)], send_a_sem.at[0])
    gather(0)

    def field_of(index, t):
        block = lanes[:, :, t * 128 : (t + 1) * 128].reshape(128, 128)
        return lax.dot_general(sep[index], block, NT, preferred_element_type=F32).astype(BF16)

    for l in range(LEVELS):
        above[l * BW : (l + 1) * BW, :] = field_of(ancestors[l, me], l)

    def couple(b, c):
        rows = pl.ds(pl.multiple_of(b * STEP, STEP), STEP)
        total[rows, :] = jnp.dot(coupling[rows, :], above[...], preferred_element_type=F32)
        return c

    lax.fori_loop(0, PHYS // STEP, couple, 0)
    for g in range(1, len(GROUPS) - 1):
        gather(g)
        first, size = GROUPS[g]
        if g == 1:
            field[...] = field_of(me, LEVELS)
            first, size = first + 1, size - 1
        wide = slice(first * 128, (first + size) * 128)
        cols = slice((first - SEPS) * 128, (first - SEPS + size) * 128)

        def add(b, c):
            rows = pl.ds(pl.multiple_of(b * STEP, STEP), STEP)
            total[rows, :] = total[rows, :] + lax.dot_general(
                modes[rows, cols],
                lanes[:, :, wide].reshape(128, wide.stop - wide.start),
                NT,
                preferred_element_type=F32,
            )
            return c

        lax.fori_loop(0, PHYS // STEP, add, 0)
    gather(len(GROUPS) - 1)
    coef_last[...] = lanes[:, :, SEPS * 128 + LAST :].reshape(128, CAP - LAST)
    for g in range(len(GROUPS)):
        settle(send_b[g].at[pl.ds(0, N_SUB - 1)], send_b_sem.at[g])


def finish(total, modes, coef, field, interior_out, field_out, interior, sem, field_sem):
    store_field = pltpu.make_async_copy(field, field_out, field_sem.at[0])
    store_field.start()

    def rows_of(b):
        return pl.ds(pl.multiple_of(b * STEP, STEP), STEP)

    def store(b):
        return pltpu.make_async_copy(
            interior.at[rows_of(b)], interior_out.at[rows_of(b)], sem.at[b]
        )

    def step(b, c):
        rows = rows_of(b)
        part = total[rows, :] + lax.dot_general(
            modes[rows, :], coef[...], NT, preferred_element_type=F32
        )
        interior[rows, :] = part.astype(BF16)
        store(b).start()
        return c

    lax.fori_loop(0, PHYS // STEP, step, 0)
    store_field.wait()
    for b in range(PHYS // STEP):
        store(b).wait()


def body(coefficients, row_counts, ancestors, interior_modes, separator_modes, coupling, pattern):
    hbm = pl.BlockSpec(memory_space=pl.ANY)
    vmem = pl.BlockSpec(memory_space=pltpu.VMEM)
    dma = pltpu.SemaphoreType.DMA
    sizes = [size for _, size in GROUPS]
    slots = [pltpu.VMEM((N_SUB, size, ROWS, 128), BF16) for size in sizes]
    results = pl.pallas_call(
        kernel,
        out_shape=(
            pltpu.VMEM((PHYS, 128), F32),
            pltpu.VMEM((PHYS, CAP - LAST), BF16),
            pltpu.VMEM((128, CAP - LAST), BF16),
            pltpu.VMEM((BW, 128), BF16),
        ),
        in_specs=[hbm] * 7,
        out_specs=(vmem,) * 4,
        scratch_shapes=[
            pltpu.SMEM((N_SUB,), jnp.int32),
            pltpu.SMEM((LEVELS, N_SUB), jnp.int32),
            pltpu.SMEM((LEVELS, 1, NBLK), jnp.int32),
            pltpu.VMEM((ROWS * N_VEC, TILES_A * 128), BF16),
            pltpu.VMEM((PHYS, LAST), BF16),
            pltpu.VMEM((N_SUB, BW, SEPM), BF16),
            pltpu.VMEM((PHYS, LEVELS * BW), BF16),
            pltpu.VMEM((N_VEC, TILES_A, ROWS, 128), BF16),
            pltpu.VMEM((TILES_I + WIN - 1, ROWS, 128), BF16),
            pltpu.VMEM((N_SUB, ROWS, 128), BF16),
            pltpu.VMEM((N_SUB // 4, 4 * ROWS, SEPS * 128 + CAP), BF16),
            pltpu.VMEM((LEVELS * BW, 128), BF16),
            dma((8,)),
            dma((1,)),
            dma((2,)),
            dma((len(sizes),)),
            dma((len(sizes),)),
            pltpu.SemaphoreType.REGULAR((5,)),
            *slots,
            *slots,
        ],
        compiler_params=pltpu.CompilerParams(
            collective_id=0, has_side_effects=True, vmem_limit_bytes=48 * 1024 * 1024
        ),
        name="recover",
    )(
        *[
            pltpu.with_memory_space_constraint(x, pltpu.HBM)
            for x in (
                row_counts,
                ancestors.T,
                jnp.transpose(pattern, (2, 0, 1)),
                coefficients,
                interior_modes,
                separator_modes.reshape(N_SUB, BW, SEPM),
                coupling,
            )
        ]
    )
    return pl.pallas_call(
        finish,
        out_shape=tuple(jax.ShapeDtypeStruct((rows, 128), BF16) for rows in (PHYS, BW)),
        in_specs=[vmem] * 4,
        out_specs=(hbm, hbm),
        scratch_shapes=[pltpu.VMEM((PHYS, 128), BF16), dma((PHYS // STEP,)), dma((1,))],
        compiler_params=pltpu.CompilerParams(vmem_limit_bytes=8 * 1024 * 1024),
        name="finish",
    )(*[pltpu.with_memory_space_constraint(x, pltpu.VMEM) for x in results])


def solution(mesh):
    placed = (P("sub", "vec"), P(), P(), P("sub", None), P(), P("sub", None), P("sub", None, None))
    return jax.shard_map(
        body,
        mesh=mesh,
        in_specs=placed,
        out_specs=(P("sub", "vec"), P("sub", "vec")),
        check_vma=False,
    )
```

```python
import jax
import jax.numpy as jnp
from jax import lax
from jax.experimental import pallas as pl
from jax.experimental.pallas import tpu as pltpu
from jax.sharding import PartitionSpec as P

BW = 256
SEPM = 128
LEVELS = 3
N_SUB = 32
N_X = 4
N_Z = 8
N_VEC = 8
ROWS = 4
TILES_A = 20
TILES_I = 128
SEPS = LEVELS + 1
WIN = 9
GROUPS = ((0, 3), (3, 4), (7, 3), (10, 2))
LAST = 6 * 128
CAP = 1024
PHYS = 4096
NBLK = PHYS // BW
STEP = 2048
MESH = pl.DeviceIdType.MESH
BF16 = jnp.bfloat16
F32 = jnp.float32
NT = (((1,), (1,)), ((), ()))


def kernel(
    counts_hbm,
    ancestors_hbm,
    gates_hbm,
    coef_hbm,
    modes_hbm,
    sep_hbm,
    coupling_hbm,
    total,
    modes_last,
    coef_last,
    field,
    counts,
    ancestors,
    gates,
    coef,
    modes,
    sep,
    coupling,
    send_a,
    recv_i,
    recv_s,
    lanes,
    above,
    load_sem,
    send_a_sem,
    recv_a_sem,
    send_b_sem,
    recv_b_sem,
    relay_sem,
    *slots,
):
    send_b = slots[: len(slots) // 2]
    recv_b = slots[len(slots) // 2 :]
    me = lax.axis_index("sub")
    mv = lax.axis_index("vec")
    mx = lax.div(me, N_Z)
    mz = lax.rem(me, N_Z)

    def along_z(d):
        return mx * N_Z + lax.rem(mz + N_Z + d, N_Z)

    def along_x(d):
        return lax.rem(mx + N_X + d, N_X) * N_Z + mz

    def load(src, dst, i):
        return pltpu.make_async_copy(src, dst, load_sem.at[i])

    load_coef = load(coef_hbm, coef, 0)
    load_sep = load(sep_hbm, sep, 1)
    load_coupling = load(coupling_hbm, coupling, 2)
    load_modes = load(modes_hbm.at[:, pl.ds(0, LAST)], modes, 3)
    load_last = load(modes_hbm.at[:, pl.ds(LAST, CAP - LAST)], modes_last, 7)
    load_counts = load(counts_hbm, counts, 4)
    load_ancestors = load(ancestors_hbm, ancestors, 5)
    load_gates = load(gates_hbm, gates, 6)

    barrier = pltpu.get_barrier_semaphore()
    for i in range(1, N_VEC):
        pl.semaphore_signal(
            barrier, inc=1, device_id={"vec": lax.rem(mv + i, N_VEC)}, device_id_type=MESH
        )
    near = [along_z(d) for d in (1, -1, 2, -2)] + [along_x(d) for d in (1, -1, 2)]
    for s in near:
        pl.semaphore_signal(barrier, inc=1, device_id={"sub": s}, device_id_type=MESH)
    load_coef.start()
    load_counts.start()
    load_ancestors.start()
    load_gates.start()
    load_coef.wait()

    def split_rows(t, c):
        cols = pl.ds(pl.multiple_of(t * 128, 128), 128)
        for v in range(N_VEC):
            send_a[v, t] = coef[ROWS * v : ROWS * (v + 1), cols]
        return c

    lax.fori_loop(0, TILES_A, split_rows, 0)
    recv_i[TILES_I:] = jnp.zeros((WIN - 1, ROWS, 128), BF16)
    pl.semaphore_wait(barrier, N_VEC - 1 + len(near))

    def tell(i, s):
        pl.semaphore_signal(relay_sem.at[i], inc=1, device_id={"sub": s}, device_id_type=MESH)

    tell(0, along_z(2))
    tell(1, along_z(-2))

    def send_rows(group, start, size):
        def own(v):
            return send_a.at[v, pl.ds(start, size)]

        there = (recv_s, recv_i)[group].at[
            pl.ds(mv * TILES_A + start - (0 if group else TILES_I), size)
        ]

        def step(i, c):
            v = lax.rem(mv + i, N_VEC)
            pltpu.make_async_remote_copy(
                src_ref=own(v),
                dst_ref=there,
                send_sem=send_a_sem.at[0],
                recv_sem=recv_a_sem.at[group],
                device_id={"vec": v},
                device_id_type=MESH,
            ).start()
            return c

        lax.fori_loop(1, N_VEC, step, 0)
        pltpu.make_async_copy(own(mv), there, recv_a_sem.at[group]).start()

    split = TILES_I // TILES_A
    cut = TILES_I - split * TILES_A

    @pl.when(mv < split)
    def _():
        send_rows(1, 0, TILES_A)

    @pl.when(mv == split)
    def _():
        send_rows(0, cut, TILES_A - cut)
        send_rows(1, 0, cut)

    @pl.when(mv > split)
    def _():
        send_rows(0, 0, TILES_A)

    def settle(ref, sem):
        pltpu.make_async_copy(ref, ref, sem).wait()

    load_sep.start()
    load_coupling.start()
    load_modes.start()
    load_last.start()
    load_counts.wait()
    load_ancestors.wait()
    load_gates.wait()
    pl.semaphore_wait(relay_sem.at[0], 1)
    pl.semaphore_wait(relay_sem.at[1], 1)
    tell(2, along_x(1))
    tell(3, along_x(-1))
    tell(4, along_x(2))
    pl.semaphore_wait(relay_sem.at[2], 1)
    pl.semaphore_wait(relay_sem.at[3], 1)
    pl.semaphore_wait(relay_sem.at[4], 1)

    def send_group(g):
        def place(j):
            h = lax.div(j + 1, 2)
            dz = (1 - 2 * lax.rem(mv, 2)) * h * (1 - 2 * lax.rem(j, 2))
            return lax.rem(mz + 12 + dz, N_Z)

        def send(z, dxs):
            for dx in dxs:
                s = lax.rem(mx + dx, N_X) * N_Z + z
                pltpu.make_async_remote_copy(
                    src_ref=send_b[g].at[s],
                    dst_ref=recv_b[g].at[me],
                    send_sem=send_b_sem.at[g],
                    recv_sem=recv_b_sem.at[g],
                    device_id={"sub": s},
                    device_id_type=MESH,
                ).start()

        def step(j, c):
            send(place(j), (2, 1, 3, 0))
            return c

        lax.fori_loop(0, 7, step, 0)
        send(mz, (2, 1, 3))
        pltpu.make_async_copy(send_b[g].at[me], recv_b[g].at[me], recv_b_sem.at[g]).start()

    settle(recv_s, recv_a_sem.at[0])
    for s in range(N_SUB):
        send_b[1][s, 0] = recv_s[s]
        for l in range(LEVELS):
            send_b[0][s, l] = recv_s[ancestors[l, s]]
    send_group(0)
    settle(recv_i.at[pl.ds(0, TILES_I)], recv_a_sem.at[1])
    offset = jnp.int32(0)
    starts = []
    for s in range(N_SUB):
        starts.append(offset)
        offset = offset + counts[s]
    for g in range(1, len(GROUPS)):
        skip = 1 if g == 1 else 0
        first = GROUPS[g][0] + skip - SEPS
        size = GROUPS[g][1] - skip
        lane = lax.broadcasted_iota(jnp.int32, (size, ROWS, 128), 2)
        place = lane + 128 * (first + lax.broadcasted_iota(jnp.int32, (size, ROWS, 128), 0))
        for s in range(N_SUB):
            shift = starts[s] & 127
            tiles = recv_i[pl.ds((starts[s] >> 7) + first, size + 1)].astype(F32)
            turned = pltpu.roll(tiles, (128 - shift) & 127, 2)
            window = jnp.where(lane < 128 - shift, turned[:size], turned[1:])
            window = jnp.where(place < counts[s], window, 0.0)
            send_b[g][s, skip:] = window.astype(BF16)
        send_group(g)

    def gather(g):
        start, size = GROUPS[g]
        settle(recv_b[g], recv_b_sem.at[g])

        def step(k, c):
            for q in range(4):
                for t in range(size):
                    cols = slice((start + t) * 128, (start + t + 1) * 128)
                    lanes[k, ROWS * q : ROWS * (q + 1), cols] = recv_b[g][k * 4 + q, t]
            return c

        lax.fori_loop(0, N_SUB // 4, step, 0)

    load_coupling.wait()

    def mask(b, c):
        rows = pl.ds(pl.multiple_of(b * BW, BW), BW)
        for l in range(LEVELS):
            cols = slice(l * BW, (l + 1) * BW)
            gate = gates[l, 0, b].astype(F32).astype(BF16)
            coupling[rows, cols] = coupling[rows, cols] * gate
        return c

    lax.fori_loop(0, NBLK, mask, 0)
    load_sep.wait()
    load_modes.wait()
    load_last.wait()
    settle(send_a.at[pl.ds(0, N_VEC - 1)], send_a_sem.at[0])
    gather(0)

    def field_of(index, t):
        block = lanes[:, :, t * 128 : (t + 1) * 128].reshape(128, 128)
        return lax.dot_general(sep[index], block, NT, preferred_element_type=F32).astype(BF16)

    for l in range(LEVELS):
        above[l * BW : (l + 1) * BW, :] = field_of(ancestors[l, me], l)

    def couple(b, c):
        rows = pl.ds(pl.multiple_of(b * STEP, STEP), STEP)
        total[rows, :] = jnp.dot(coupling[rows, :], above[...], preferred_element_type=F32)
        return c

    lax.fori_loop(0, PHYS // STEP, couple, 0)
    for g in range(1, len(GROUPS) - 1):
        gather(g)
        first, size = GROUPS[g]
        if g == 1:
            field[...] = field_of(me, LEVELS)
            first, size = first + 1, size - 1
        wide = slice(first * 128, (first + size) * 128)
        cols = slice((first - SEPS) * 128, (first - SEPS + size) * 128)

        def add(b, c):
            rows = pl.ds(pl.multiple_of(b * STEP, STEP), STEP)
            total[rows, :] = total[rows, :] + lax.dot_general(
                modes[rows, cols],
                lanes[:, :, wide].reshape(128, wide.stop - wide.start),
                NT,
                preferred_element_type=F32,
            )
            return c

        lax.fori_loop(0, PHYS // STEP, add, 0)
    gather(len(GROUPS) - 1)
    coef_last[...] = lanes[:, :, SEPS * 128 + LAST :].reshape(128, CAP - LAST)
    for g in range(len(GROUPS)):
        settle(send_b[g].at[pl.ds(0, N_SUB - 1)], send_b_sem.at[g])


def finish(total, modes, coef, field, interior_out, field_out, interior, sem, field_sem):
    store_field = pltpu.make_async_copy(field, field_out, field_sem.at[0])
    store_field.start()

    def rows_of(b):
        return pl.ds(pl.multiple_of(b * STEP, STEP), STEP)

    def store(b):
        return pltpu.make_async_copy(
            interior.at[rows_of(b)], interior_out.at[rows_of(b)], sem.at[b]
        )

    def step(b, c):
        rows = rows_of(b)
        part = total[rows, :] + lax.dot_general(
            modes[rows, :], coef[...], NT, preferred_element_type=F32
        )
        interior[rows, :] = part.astype(BF16)
        store(b).start()
        return c

    lax.fori_loop(0, PHYS // STEP, step, 0)
    store_field.wait()
    for b in range(PHYS // STEP):
        store(b).wait()


def body(coefficients, row_counts, ancestors, interior_modes, separator_modes, coupling, pattern):
    hbm = pl.BlockSpec(memory_space=pl.ANY)
    vmem = pl.BlockSpec(memory_space=pltpu.VMEM)
    dma = pltpu.SemaphoreType.DMA
    sizes = [size for _, size in GROUPS]
    slots = [pltpu.VMEM((N_SUB, size, ROWS, 128), BF16) for size in sizes]
    results = pl.pallas_call(
        kernel,
        out_shape=(
            pltpu.VMEM((PHYS, 128), F32),
            pltpu.VMEM((PHYS, CAP - LAST), BF16),
            pltpu.VMEM((128, CAP - LAST), BF16),
            pltpu.VMEM((BW, 128), BF16),
        ),
        in_specs=[hbm] * 7,
        out_specs=(vmem,) * 4,
        scratch_shapes=[
            pltpu.SMEM((N_SUB,), jnp.int32),
            pltpu.SMEM((LEVELS, N_SUB), jnp.int32),
            pltpu.SMEM((LEVELS, 1, NBLK), jnp.int32),
            pltpu.VMEM((ROWS * N_VEC, TILES_A * 128), BF16),
            pltpu.VMEM((PHYS, LAST), BF16),
            pltpu.VMEM((N_SUB, BW, SEPM), BF16),
            pltpu.VMEM((PHYS, LEVELS * BW), BF16),
            pltpu.VMEM((N_VEC, TILES_A, ROWS, 128), BF16),
            pltpu.VMEM((TILES_I + WIN - 1, ROWS, 128), BF16),
            pltpu.VMEM((N_SUB, ROWS, 128), BF16),
            pltpu.VMEM((N_SUB // 4, 4 * ROWS, SEPS * 128 + CAP), BF16),
            pltpu.VMEM((LEVELS * BW, 128), BF16),
            dma((8,)),
            dma((1,)),
            dma((2,)),
            dma((len(sizes),)),
            dma((len(sizes),)),
            pltpu.SemaphoreType.REGULAR((5,)),
            *slots,
            *slots,
        ],
        compiler_params=pltpu.CompilerParams(
            collective_id=0, has_side_effects=True, vmem_limit_bytes=48 * 1024 * 1024
        ),
        name="recover",
    )(
        *[
            pltpu.with_memory_space_constraint(x, pltpu.HBM)
            for x in (
                row_counts,
                ancestors.T,
                jnp.transpose(pattern, (2, 0, 1)),
                coefficients,
                interior_modes,
                separator_modes.reshape(N_SUB, BW, SEPM),
                coupling,
            )
        ]
    )
    return pl.pallas_call(
        finish,
        out_shape=tuple(jax.ShapeDtypeStruct((rows, 128), BF16) for rows in (PHYS, BW)),
        in_specs=[vmem] * 4,
        out_specs=(hbm, hbm),
        scratch_shapes=[pltpu.VMEM((PHYS, 128), BF16), dma((PHYS // STEP,)), dma((1,))],
        compiler_params=pltpu.CompilerParams(vmem_limit_bytes=8 * 1024 * 1024),
        name="finish",
    )(*[pltpu.with_memory_space_constraint(x, pltpu.VMEM) for x in results])


def solution(mesh):
    placed = (P("sub", "vec"), P(), P(), P("sub", None), P(), P("sub", None), P("sub", None, None))
    return jax.shard_map(
        body,
        mesh=mesh,
        in_specs=placed,
        out_specs=(P("sub", "vec"), P("sub", "vec")),
        check_vma=False,
    )
```
